128 devices in a mesh: member: 4 (over z), region: 32 (over y, x, core).
Axes of the slice: x: 4, y: 4, z: 4, core: 2. Of those that a mesh axis runs over, the one named last changes fastest.
Arguments:
- grid_input: bfloat16 [16, 16384, 1024], P('member', 'region'), may hold values from -6 to 6
- w_hidden: bfloat16 [1024, 1024], replicated, may hold values from -0.1875 to 0.1875
- b_hidden: float32 [1024], replicated, may hold values from -3 to 3
- w_out: bfloat16 [1024, 96], replicated, may hold values from -0.1875 to 0.1875
- b_out: float32 [96], replicated, may hold values from -3 to 3
- target: float32 [96, 16384], P(None, 'region'), may hold values from -6 to 6
- channel_weight: float32 [96], replicated, may hold values from 0.5 to 5
- interp_weight: bfloat16 [128, 3, 128, 128], P('region'), may hold values from -0.5 to 0.5
- block_index: int32 [128, 3], P('region'), may hold values from 0 to 63, as said below
Outputs:
- grad_w_hidden: float32 [1024, 1024], P(('member', 'region'))
- grad_w_out: float32 [1024, 96], P(('member', 'region'))
- grad_mesh: float32 [16, 8192, 1024], P('member', 'region')
The draws below stay inside these ranges and needn't reach their ends.
Inputs may be any that keep to these rules, and one draw needn't show every extreme that they name: `block_index`: grid block b lies in region b // 4; its mesh blocks belong to that region or to one of its two neighbours along the region index, cyclically, a block j belonging to region j // 2. For k = 0 the mesh block is the region's own block number (b % 4) % 2.
All inputs are finite; a program needn't handle non-finite values.
Results may differ from the reference program's by a relative error of at most 0.0095.
Values may be sent and summed in bfloat16 or wider, within the bound.
A program may use at most 128 MiB of HBM per device.

```python
import math
import jax
import jax.numpy as jnp
from jax import lax

M = 16
H = 1024
C = 96
GB = 128
MB = 128
K = 3
GBLK_REG = 4
MBLK_REG = 2
NGB = 128
NMB = 64
NCELL = 16384
NMESH = 8192


def draw_block_index(key, part):
    position = jnp.arange(NGB, dtype=jnp.int32)
    region_of = position // GBLK_REG
    local_pos = position % GBLK_REG
    regions = NMB // MBLK_REG
    key_offset, key_within = jax.random.split(key)
    offset = jax.random.randint(key_offset, (NGB, K), -1, 2).astype(jnp.int32)
    within = jax.random.randint(key_within, (NGB, K), 0, MBLK_REG).astype(jnp.int32)
    first = (jnp.arange(K, dtype=jnp.int32) == 0)[None, :]
    offset = jnp.where(first, 0, offset)
    within = jnp.where(first, (local_pos % MBLK_REG)[:, None], within)
    owner = (region_of[:, None] + offset + regions) % regions
    return (owner * MBLK_REG + within).astype(jnp.int32)


def steps_of(own_key, extent, pieces, low, high):
    level = 1.0
    for dim, parts in pieces:
        draws = jax.random.uniform(jax.random.fold_in(jax.random.fold_in(own_key, 6), dim), (parts,), jnp.float32, low / len(pieces), high / len(pieces))
        level = level * jnp.repeat(jnp.exp(draws), extent[dim] // parts).reshape((-1,) + (1,) * (len(extent) - 1 - dim))
    return level


def centred(key, shape, scale, reach, pieces=(), kind=jnp.bfloat16):
    gain = steps_of(key, shape, pieces, -0.22, 0.18) if pieces else 1.0
    entries = jax.random.normal(key, shape, jnp.float32) * scale * gain
    return jnp.minimum(jnp.maximum(entries, -reach), reach).astype(kind)


def setup_inputs(seed: int = 0) -> dict:
    seeds = jax.random.split(jax.random.key(seed), 10)
    return {
        "grid_input": centred(seeds[0], (M, NCELL, H), 1.0, 6.0, ((0, 4), (1, 32))),
        "w_hidden": centred(seeds[1], (H, H), H ** -0.5, 0.1875),
        "b_hidden": centred(seeds[2], (H,), 0.5, 3.0, (), jnp.float32),
        "w_out": centred(seeds[3], (H, C), H ** -0.5, 0.1875),
        "b_out": centred(seeds[4], (C,), 0.5, 3.0, (), jnp.float32),
        "target": centred(seeds[5], (C, NCELL), 1.0, 6.0, ((1, 32),), jnp.float32),
        "channel_weight": jnp.clip(jnp.exp(jax.random.uniform(seeds[6], (C,), jnp.float32, math.log(0.5), math.log(5.0))), 0.5, 5.0),
        "interp_weight": centred(seeds[7], (NGB, K, GB, MB), MB ** -0.5, 0.5, ((0, 32),)),
        "block_index": draw_block_index(jax.random.fold_in(seeds[9], 71), 0),
    }


ALPHA = 0.95
SMOOTH = 0.25

def smooth_slope(diff):
    return diff / jnp.sqrt(diff * diff + SMOOTH * SMOOTH)

def ensemble_adjoint(own, every, target_cells, channel_weight):
    members = every.shape[0]
    kappa = ALPHA / (2.0 * members * (members - 1)) + (1.0 - ALPHA) / (2.0 * members * members)
    skill = smooth_slope(own - target_cells[None]) / members
    spread = lax.optimization_barrier(jnp.sum(smooth_slope(own[:, None] - every[None, :]), axis=1))
    return channel_weight[None, :, None] * (skill - 2.0 * kappa * spread)

def reference(grid_input, w_hidden, b_hidden, w_out, b_out, target, channel_weight, interp_weight, block_index):

    def forward(member_input):
        pre_act = jnp.dot(member_input, w_hidden, preferred_element_type=jnp.float32) + b_hidden
        activated = jax.nn.silu(pre_act).astype(jnp.bfloat16)
        return jnp.dot(activated, w_out, preferred_element_type=jnp.float32) + b_out
    predicted = lax.map(forward, grid_input)
    pred_blocks = predicted.reshape(M, NGB, GB, C).transpose(1, 0, 3, 2)
    target_blocks = target.reshape(C, NGB, GB).transpose(1, 0, 2)

    def score_block(pair):
        return ensemble_adjoint(pair[0], pair[0], pair[1], channel_weight)
    adjoint = lax.map(score_block, (pred_blocks, target_blocks))
    dpred_all = adjoint.astype(jnp.bfloat16).transpose(1, 0, 3, 2).reshape(M, NCELL, C)
    tiles = interp_weight.astype(jnp.float32)
    flat_index = block_index.reshape(-1).astype(jnp.int32)

    def backward(pair):
        member_input, member_dpred = pair
        pre_act = jnp.dot(member_input, w_hidden, preferred_element_type=jnp.float32) + b_hidden
        activated = jax.nn.silu(pre_act).astype(jnp.bfloat16)
        dact = jnp.dot(member_dpred, w_out.T, preferred_element_type=jnp.float32)
        logistic = jax.nn.sigmoid(pre_act)
        dpre = (dact * logistic * (1.0 + pre_act * (1.0 - logistic))).astype(jnp.bfloat16)
        dinput = jnp.dot(dpre, w_hidden.T, preferred_element_type=jnp.float32).astype(jnp.bfloat16)
        grad_hidden = jnp.dot(member_input.T, dpre, preferred_element_type=jnp.float32)
        grad_output = jnp.dot(activated.T, member_dpred, preferred_element_type=jnp.float32)
        blocks = dinput.reshape(NGB, GB, H).astype(jnp.float32)
        contrib = jnp.einsum('bkgn,bgh->bknh', tiles, blocks, precision=lax.Precision.HIGHEST)
        mesh = jax.ops.segment_sum(contrib.reshape(NGB * K, MB, H), flat_index, num_segments=NMB)
        return (grad_hidden, grad_output, mesh.reshape(NMESH, H))
    grads_hidden, grads_output, grad_mesh = lax.map(backward, (grid_input, dpred_all))
    return (lax.optimization_barrier(jnp.sum(grads_hidden, axis=0)), lax.optimization_barrier(jnp.sum(grads_output, axis=0)), grad_mesh)
```

```python
import jax
import jax.numpy as jnp
from jax import lax
from jax.experimental import pallas as pl
from jax.experimental.pallas import tpu as pltpu
from jax.sharding import PartitionSpec as P

MESH = pl.DeviceIdType.MESH
F32 = jnp.float32
BF16 = jnp.bfloat16
M = 16
ALPHA = 0.95
SMOOTH = 0.25
KAPPA = ALPHA / (2.0 * M * (M - 1)) + (1.0 - ALPHA) / (2.0 * M * M)
CA = 640
CW = 1152


def kernel(
    x_hbm, wh_hbm, wot_hbm, bh_ref, bo_ref, cw_ref, tgt_hbm, tile_hbm, bi_ref,
    gh_ref, go_ref, mesh_hbm,
    xv, wh, wot, tiles, tgt, act, dsil, dpre, wt, bcol, ccol,
    predsend, predrecv, pf, adjf, adjsend, adjrecv, outt,
    own, send_dn, send_up, recv_dn, recv_up,
    accf, csend, crecv, s1a, s1b, r1a, r1b, p2a, p2b, s2a, s2b, r2a, r2b, p3, r3,
    load_sem, x_sem, pred_ss, pred_rs, adj_ss, adj_rs, dn_ss, dn_rs, up_ss, up_rs,
    c_ss, c_rs, a1_ss, a1_rs, b1_ss, b1_rs, a2_ss, a2_rs, b2_ss, b2_rs, x_ss, x_rs, out_sem,
):
    z = lax.axis_index("member")
    r = lax.axis_index("region")
    yy, xx, cc = r // 8, (r // 2) % 4, r % 2
    oc = 1 - cc

    def zdev(k):
        return ((z + k) % 4, r)

    def ydev(k):
        return (z, ((yy + k) % 4) * 8 + xx * 2 + cc)

    def xdev(k):
        return (z, yy * 8 + ((xx + k) % 4) * 2 + cc)

    partner = (z, r + 1 - 2 * cc)
    up = (z, (r + 1) % 32)
    down = (z, (r + 31) % 32)

    def block_of(i):
        return (z + 1 + i) % 4

    load_wh = pltpu.make_async_copy(wh_hbm, wh, load_sem.at[0])
    load_wh.start()

    def x_copy(i):
        start = pl.multiple_of(block_of(i) * 128, 128)
        return pltpu.make_async_copy(
            x_hbm.at[:, pl.ds(start, 128), :], xv.at[i], x_sem.at[i]
        )

    x_copy(0).start()
    load_wot = pltpu.make_async_copy(wot_hbm, wot, load_sem.at[1])
    load_wot.start()
    for i in range(1, 4):
        x_copy(i).start()
    load_tiles = pltpu.make_async_copy(tile_hbm, tiles, load_sem.at[2])
    load_tiles.start()
    load_tgt = pltpu.make_async_copy(
        tgt_hbm.at[:, pl.ds(pl.multiple_of(z * 128, 128), 128)], tgt, load_sem.at[3]
    )
    load_tgt.start()

    barrier = pltpu.get_barrier_semaphore()
    peers = [f(k) for f in (zdev, ydev, xdev) for k in (1, 2, 3)] + [up, down]
    for peer in peers:
        pl.semaphore_signal(barrier, inc=1, device_id=peer, device_id_type=MESH)
    pl.semaphore_wait(barrier, len(peers))

    def pred_copy(i):
        return pltpu.make_async_remote_copy(
            src_ref=predsend.at[i], dst_ref=predrecv.at[i],
            send_sem=pred_ss.at[i], recv_sem=pred_rs.at[i],
            device_id=zdev(i + 1), device_id_type=MESH,
        )

    load_wh.wait()
    load_wot.wait()

    def forward(i, carry):
        x_copy(i).wait()
        xb = xv[i].reshape(512, 1024)
        for n in range(4):
            cols = slice(n * 256, n * 256 + 256)
            pre = jnp.dot(xb, wh[:, cols], preferred_element_type=F32) + bh_ref[:, cols]
            sig = 0.5 + 0.5 * jnp.tanh(0.5 * pre)
            silu = pre * sig
            act[i, :, :, cols] = silu.astype(BF16).reshape(4, 128, 256)
            dsil[i, :, :, cols] = (sig + silu * (1.0 - sig)).reshape(4, 128, 256)
        predt = lax.dot_general(
            wot[...], act[i].reshape(512, 1024), (((1,), (1,)), ((), ())),
            preferred_element_type=F32,
        ).astype(BF16)
        for m in range(4):
            predsend[i, m] = predt[:, m * 128 : m * 128 + 128]

        @pl.when(i < 3)
        def _():
            pred_copy(i).start()

        return carry

    lax.fori_loop(0, 4, forward, 0)

    load_tiles.wait()

    def build(i, carry):
        b = block_of(i)
        slots = []
        turned = []
        for k in range(3):
            index = bi_ref[b, k]
            relative = (index // 2 - r + 33) % 32
            slots.append(relative * 2 + index % 2)
            turned.append(tiles[b, k].astype(F32).T)
        for s in range(6):
            total = None
            for k in range(3):
                term = turned[k] * jnp.where(slots[k] == s, 1.0, 0.0)
                total = term if total is None else total + term
            wt[i, s * 128 : s * 128 + 128, :] = total.astype(BF16)
        return carry

    lax.fori_loop(0, 4, build, 0)

    bcol[...] = jnp.zeros_like(bcol)
    ccol[...] = jnp.zeros_like(ccol)
    bcol[:, :96] = jnp.broadcast_to(bo_ref[...], (128, 96))
    ccol[:, :96] = jnp.broadcast_to(cw_ref[...], (128, 96))
    bcol[...] = bcol[...].T
    ccol[...] = ccol[...].T
    load_tgt.wait()

    pf[12:16] = predsend[3].astype(F32)
    for i in range(3):
        pred_copy(i).wait_recv()
        pf[4 * i : 4 * i + 4] = predrecv[i].astype(F32)

    def score(t, carry):
        rows = pl.ds(pl.multiple_of(t * 8, 8), 8)
        p = pf[:, rows, :]
        aim = tgt[rows, :] - bcol[rows, :]

        def slope(d):
            return d * lax.rsqrt(d * d + SMOOTH * SMOOTH)

        spread = None
        for k in range(1, 8):
            s = slope(p - jnp.concatenate([p[k:], p[:k]], axis=0))
            change = s - jnp.concatenate([s[16 - k :], s[: 16 - k]], axis=0)
            spread = change if spread is None else spread + change
        s = slope(p[:8] - p[8:])
        spread = spread + jnp.concatenate([s, -s], axis=0)
        skill = slope(p - aim[None])
        adjf[:, rows, :] = ccol[rows, :][None] * (skill * (1.0 / M) - 2.0 * KAPPA * spread)
        return carry

    lax.fori_loop(0, 12, score, 0)

    def adj_copy(m, i):
        return pltpu.make_async_remote_copy(
            src_ref=adjsend.at[m, i], dst_ref=adjrecv.at[m, i],
            send_sem=adj_ss.at[m, i], recv_sem=adj_rs.at[m, i],
            device_id=zdev(3 - i), device_id_type=MESH,
        )

    for m in range(4):
        for i in range(3):
            adjsend[m, i] = adjf[4 * i + m].astype(BF16)
            adj_copy(m, i).start()
        adjrecv[m, 3] = adjf[12 + m].astype(BF16)

    def dn_copy(m):
        return pltpu.make_async_remote_copy(
            src_ref=send_dn.at[m], dst_ref=recv_dn.at[m],
            send_sem=dn_ss.at[m], recv_sem=dn_rs.at[m],
            device_id=down, device_id_type=MESH,
        )

    def up_copy(m):
        return pltpu.make_async_remote_copy(
            src_ref=send_up.at[m], dst_ref=recv_up.at[m],
            send_sem=up_ss.at[m], recv_sem=up_rs.at[m],
            device_id=up, device_id_type=MESH,
        )

    outt[...] = jnp.zeros_like(outt)

    def backward(m, carry):
        for i in range(3):
            adj_copy(m, i).wait_recv()
        adj = jnp.concatenate([adjrecv[m, i] for i in range(4)], axis=1)
        for n in range(4):
            cols = slice(n * 256, n * 256 + 256)
            dact = lax.dot_general(
                adj, wot[:, cols], (((0,), (0,)), ((), ())), preferred_element_type=F32
            )
            grad = dact * dsil[:, m, :, cols].reshape(512, 256)
            dpre[:, m, :, cols] = grad.astype(BF16).reshape(4, 128, 256)
        outt[:96, :] += jnp.dot(
            adj, act[:, m].reshape(512, 1024), preferred_element_type=F32
        )
        dp = dpre[:, m].reshape(512, 1024)
        lhs = jnp.concatenate([wt[i] for i in range(4)], axis=1)
        for n in range(4):
            cols = slice(n * 256, n * 256 + 256)
            dinput = lax.dot_general(
                dp, wh[cols, :], (((1,), (1,)), ((), ())), preferred_element_type=F32
            ).astype(BF16)
            contrib = jnp.dot(lhs, dinput, preferred_element_type=F32)
            send_dn[m, :, cols] = contrib[:256].astype(BF16)
            own[m, :, cols] = contrib[256:512]
            send_up[m, :, cols] = contrib[512:].astype(BF16)
        dn_copy(m).start()
        up_copy(m).start()
        return carry

    lax.fori_loop(0, 4, backward, 0)

    turned_out = outt[...].T.reshape(4, 4, 4, 2, 8, 128)
    for c in range(2):
        accf[c, :, :, :, 1024:] = turned_out[:, :, :, c].reshape(4, 4, 32, 128)

    def c_copy(zc):
        return pltpu.make_async_remote_copy(
            src_ref=csend.at[zc], dst_ref=crecv.at[zc],
            send_sem=c_ss.at[zc], recv_sem=c_rs.at[zc],
            device_id=partner, device_id_type=MESH,
        )

    def weights(zc, carry):
        start = pl.multiple_of(zc * 256, 256)
        lhs = xv[:, :, :, pl.ds(start, 256)].reshape(2048, 256)
        for n in range(2):
            cols = slice(n * 512, n * 512 + 512)
            part = lax.dot_general(
                lhs, dpre[:, :, :, cols].reshape(2048, 512), (((0,), (0,)), ((), ())),
                preferred_element_type=F32,
            ).reshape(4, 4, 2, 8, 512)
            for c in range(2):
                accf[c, zc, :, :, cols] = part[:, :, c].reshape(4, 32, 512)
        csend[zc] = accf[oc, zc].astype(BF16)
        c_copy(zc).start()
        return carry

    lax.fori_loop(0, 4, weights, 0)

    def combine(zc, carry):
        c_copy(zc).wait_recv()
        total = accf[cc, zc] + crecv[zc].astype(F32)
        accf[cc, zc] = total
        s1a[zc] = total[:, :, :CA].astype(BF16)
        s1b[:, zc] = total[:, :, CA:].astype(BF16)
        return carry

    lax.fori_loop(0, 4, combine, 0)

    def remote(src, dst, ss, rs, dev, k):
        return pltpu.make_async_remote_copy(
            src_ref=src, dst_ref=dst, send_sem=ss.at[k - 1], recv_sem=rs.at[k - 1],
            device_id=dev, device_id_type=MESH,
        )

    def a1(k):
        return remote(s1a.at[(z + k) % 4], r1a.at[k - 1], a1_ss, a1_rs, zdev(k), k)

    def b1(k):
        return remote(s1b.at[(yy + k) % 4], r1b.at[k - 1], b1_ss, b1_rs, ydev(k), k)

    def a2(k):
        return remote(s2a.at[(yy + k) % 4], r2a.at[k - 1], a2_ss, a2_rs, ydev(k), k)

    def b2(k):
        return remote(s2b.at[(z + k) % 4], r2b.at[k - 1], b2_ss, b2_rs, zdev(k), k)

    def x3(k):
        return remote(p3.at[(xx + k) % 4], r3.at[k - 1], x_ss, x_rs, xdev(k), k)

    for k in (2, 1, 3):
        a1(k).start()
        b1(k).start()

    def out_copy(m):
        return pltpu.make_async_copy(own.at[m], mesh_hbm.at[m], out_sem.at[m])

    def finish(m, carry):
        dn_copy(m).wait_recv()
        up_copy(m).wait_recv()
        own[m] = own[m] + recv_dn[m].astype(F32) + recv_up[m].astype(F32)
        out_copy(m).start()
        return carry

    lax.fori_loop(0, 2, finish, 0)

    for k in (1, 3, 2):
        a1(k).wait_recv()
    total = accf[cc, z, :, :, :CA]
    for k in range(3):
        total = total + r1a[k].astype(F32)
    p2a[...] = total
    s2a[...] = total.astype(BF16)
    for k in (2, 1, 3):
        a2(k).start()
    for k in (1, 3, 2):
        b1(k).wait_recv()
    total = accf[cc, :, yy, :, CA:]
    for k in range(3):
        total = total + r1b[k].astype(F32)
    p2b[...] = total
    s2b[...] = total.astype(BF16)
    for k in (2, 1, 3):
        b2(k).start()

    lax.fori_loop(2, 3, finish, 0)

    for k in (1, 3, 2):
        a2(k).wait_recv()
    total = p2a[yy]
    for k in range(3):
        total = total + r2a[k].astype(F32)
    p3[:, :, :CA] = total.reshape(4, 8, CA)
    for k in (1, 3, 2):
        b2(k).wait_recv()
    total = p2b[z]
    for k in range(3):
        total = total + r2b[k].astype(F32)
    p3[:, :, CA:] = total.reshape(4, 8, CW - CA)
    for k in (2, 1, 3):
        x3(k).start()
    for k in (1, 3, 2):
        x3(k).wait_recv()
    total = p3[xx]
    for k in range(3):
        total = total + r3[k]
    gh_ref[...] = total[:, :1024]
    go_ref[...] = total[:, 1024:]

    lax.fori_loop(3, 4, finish, 0)

    for i in range(3):
        pred_copy(i).wait_send()
        for m in range(4):
            adj_copy(m, i).wait_send()
    for m in range(4):
        dn_copy(m).wait_send()
        up_copy(m).wait_send()
        c_copy(m).wait_send()
        out_copy(m).wait()
    for k in (1, 2, 3):
        for f in (a1, b1, a2, b2, x3):
            f(k).wait_send()


def body(
    grid_input, w_hidden, b_hidden, w_out, b_out, target, channel_weight, interp_weight, block_index
):
    V = pltpu.VMEM
    D = pltpu.SemaphoreType.DMA
    any_spec = pl.BlockSpec(memory_space=pl.ANY)
    vmem_spec = pl.BlockSpec(memory_space=pltpu.VMEM)
    scratch = [
        V((4, 4, 128, 1024), BF16), V((1024, 1024), BF16), V((96, 1024), BF16),
        V((4, 3, 128, 128), BF16), V((96, 128), F32),
        V((4, 4, 128, 1024), BF16), V((4, 4, 128, 1024), F32), V((4, 4, 128, 1024), BF16),
        V((4, 768, 128), BF16), V((128, 128), F32), V((128, 128), F32),
        V((4, 4, 96, 128), BF16), V((3, 4, 96, 128), BF16),
        V((16, 96, 128), F32), V((16, 96, 128), F32),
        V((4, 3, 96, 128), BF16), V((4, 4, 96, 128), BF16), V((128, 1024), F32),
        V((4, 256, 1024), F32),
        V((4, 256, 1024), BF16), V((4, 256, 1024), BF16),
        V((4, 256, 1024), BF16), V((4, 256, 1024), BF16),
        V((2, 4, 4, 32, CW), F32), V((4, 4, 32, CW), BF16), V((4, 4, 32, CW), BF16),
        V((4, 4, 32, CA), BF16), V((4, 4, 32, CW - CA), BF16),
        V((3, 4, 32, CA), BF16), V((3, 4, 32, CW - CA), BF16),
        V((4, 32, CA), F32), V((4, 32, CW - CA), F32),
        V((4, 32, CA), BF16), V((4, 32, CW - CA), BF16),
        V((3, 32, CA), BF16), V((3, 32, CW - CA), BF16),
        V((4, 8, CW), F32), V((3, 8, CW), F32),
        D((4,)), D((4,)), D((3,)), D((3,)), D((4, 3)), D((4, 3)),
        D((4,)), D((4,)), D((4,)), D((4,)), D((4,)), D((4,)),
        D((3,)), D((3,)), D((3,)), D((3,)), D((3,)), D((3,)), D((3,)), D((3,)),
        D((3,)), D((3,)), D((4,)),
    ]
    grad_hidden, grad_out, grad_mesh = pl.pallas_call(
        kernel,
        out_shape=(
            jax.ShapeDtypeStruct((8, 1024), F32),
            jax.ShapeDtypeStruct((8, 128), F32),
            jax.ShapeDtypeStruct((4, 256, 1024), F32),
        ),
        in_specs=[any_spec] * 3 + [vmem_spec] * 3 + [any_spec] * 2
        + [pl.BlockSpec(memory_space=pltpu.SMEM)],
        out_specs=(vmem_spec, vmem_spec, any_spec),
        scratch_shapes=scratch,
        compiler_params=pltpu.CompilerParams(
            collective_id=0, has_side_effects=True, vmem_limit_bytes=60 * 1024 * 1024
        ),
    )(
        grid_input, w_hidden, w_out.T, b_hidden[None], b_out[None], channel_weight[None],
        target, interp_weight, block_index,
    )
    return grad_hidden, grad_out[:, :96], grad_mesh


def solution(mesh):
    placed = (
        P("member", "region", None),
        P(),
        P(),
        P(),
        P(),
        P(None, "region"),
        P(),
        P("region", None, None, None),
        P("region", None),
    )
    return jax.shard_map(
        body,
        mesh=mesh,
        in_specs=placed,
        out_specs=(
            P(("member", "region"), None),
            P(("member", "region"), None),
            P("member", "region", None),
        ),
        check_vma=False,
    )
```

```python
import jax
import jax.numpy as jnp
from jax import lax
from jax.experimental import pallas as pl
from jax.experimental.pallas import tpu as pltpu
from jax.sharding import PartitionSpec as P

MESH = pl.DeviceIdType.MESH
F32 = jnp.float32
BF16 = jnp.bfloat16
M = 16
ALPHA = 0.95
SMOOTH = 0.25
KAPPA = ALPHA / (2.0 * M * (M - 1)) + (1.0 - ALPHA) / (2.0 * M * M)
CA = 640
CW = 1152


def kernel(
    x_hbm, wh_hbm, wot_hbm, bh_ref, bo_ref, cw_ref, tgt_hbm, tile_hbm, bi_ref,
    gh_ref, go_ref, own,
    xv, wh, wht, wot, wo, tiles, tgt, act, dsil, dpre, wt, bcol, ccol,
    predsend, predrecv, pf, adjf, adjsend, adjrecv, outt,
    send_dn, send_up, recv_dn, recv_up,
    accf, csend, crecv, s1a, s1b, r1a, r1b, p2a, p2b, s2a, s2b, r2a, r2b, p3, r3,
    load_sem, x_sem, pred_ss, pred_rs, adj_ss, adj_rs, dn_ss, dn_rs, up_ss, up_rs,
    c_ss, c_rs, a1_ss, a1_rs, b1_ss, b1_rs, a2_ss, a2_rs, b2_ss, b2_rs, x_ss, x_rs,
):
    z = lax.axis_index("member")
    r = lax.axis_index("region")
    yy, xx, cc = r // 8, (r // 2) % 4, r % 2
    oc = 1 - cc

    def zdev(k):
        return ((z + k) % 4, r)

    def ydev(k):
        return (z, ((yy + k) % 4) * 8 + xx * 2 + cc)

    def xdev(k):
        return (z, yy * 8 + ((xx + k) % 4) * 2 + cc)

    partner = (z, r + 1 - 2 * cc)
    up = (z, (r + 1) % 32)
    down = (z, (r + 31) % 32)

    def block_of(i):
        return (z + 1 + i) % 4

    barrier = pltpu.get_barrier_semaphore()
    peers = [f(k) for f in (zdev, ydev, xdev) for k in (1, 2, 3)] + [up, down]
    for peer in peers:
        pl.semaphore_signal(barrier, inc=1, device_id=peer, device_id_type=MESH)

    load_wh = pltpu.make_async_copy(wh_hbm, wh, load_sem.at[0])
    load_wh.start()

    def x_copy(i):
        start = pl.multiple_of(block_of(i) * 128, 128)
        return pltpu.make_async_copy(
            x_hbm.at[:, pl.ds(start, 128), :], xv.at[i], x_sem.at[i]
        )

    x_copy(0).start()
    load_wot = pltpu.make_async_copy(wot_hbm, wot.at[:96], load_sem.at[1])
    load_wot.start()
    for i in range(1, 4):
        x_copy(i).start()
    load_tiles = pltpu.make_async_copy(tile_hbm, tiles, load_sem.at[2])
    load_tiles.start()
    load_tgt = pltpu.make_async_copy(
        tgt_hbm.at[:, pl.ds(pl.multiple_of(z * 128, 128), 128)], tgt, load_sem.at[3]
    )
    load_tgt.start()

    def pred_copy(i):
        return pltpu.make_async_remote_copy(
            src_ref=predsend.at[i], dst_ref=predrecv.at[i],
            send_sem=pred_ss.at[i], recv_sem=pred_rs.at[i],
            device_id=zdev(i + 1), device_id_type=MESH,
        )

    wot[96:] = jnp.zeros((32, 1024), BF16)
    load_wot.wait()
    wo[...] = wot[...].T
    load_wh.wait()

    def forward(i, carry):
        x_copy(i).wait()
        xb = xv[i].reshape(512, 1024)
        for n in range(4):
            cols = slice(n * 256, n * 256 + 256)
            pre = jnp.dot(xb, wh[:, cols], preferred_element_type=F32) + bh_ref[:, cols]
            sig = 0.5 + 0.5 * jnp.tanh(0.5 * pre)
            silu = pre * sig
            act[i, :, :, cols] = silu.astype(BF16).reshape(4, 128, 256)
            dsil[i, :, :, cols] = (sig + silu * (1.0 - sig)).reshape(4, 128, 256)
        predt = jnp.dot(
            act[i].reshape(512, 1024), wo[...], preferred_element_type=F32
        ).T.astype(BF16)
        for m in range(4):
            predsend[i, m] = predt[:96, m * 128 : m * 128 + 128]

        @pl.when(i == 0)
        def _():
            pl.semaphore_wait(barrier, len(peers))

        @pl.when(i < 3)
        def _():
            pred_copy(i).start()

        return carry

    lax.fori_loop(0, 4, forward, 0)

    load_tiles.wait()

    def build(i, carry):
        b = block_of(i)
        place = pl.ds(pl.multiple_of(i * 128, 128), 128)
        slots = []
        turned = []
        for k in range(3):
            index = bi_ref[b, k]
            relative = (index // 2 - r + 33) % 32
            slots.append(relative * 2 + index % 2)
            turned.append(tiles[b, k].astype(F32).T)
        for s in range(6):
            total = None
            for k in range(3):
                term = turned[k] * jnp.where(slots[k] == s, 1.0, 0.0)
                total = term if total is None else total + term
            wt[s * 128 : s * 128 + 128, place] = total.astype(BF16)
        return carry

    lax.fori_loop(0, 4, build, 0)

    for n in range(4):
        wht[:, n * 256 : n * 256 + 256] = wh[n * 256 : n * 256 + 256, :].T

    bcol[...] = jnp.zeros_like(bcol)
    ccol[...] = jnp.zeros_like(ccol)
    bcol[:, :96] = jnp.broadcast_to(bo_ref[...], (128, 96))
    ccol[:, :96] = jnp.broadcast_to(cw_ref[...], (128, 96))
    bcol[...] = bcol[...].T
    ccol[...] = ccol[...].T
    load_tgt.wait()

    pf[12:16] = predsend[3].astype(F32)
    for i in range(3):
        pred_copy(i).wait_recv()
        pf[4 * i : 4 * i + 4] = predrecv[i].astype(F32)

    def score(t, carry):
        rows = pl.ds(pl.multiple_of(t * 8, 8), 8)
        p = pf[:, rows, :]
        aim = tgt[rows, :] - bcol[rows, :]

        def slope(d):
            return d * lax.rsqrt(d * d + SMOOTH * SMOOTH)

        spread = None
        for k in range(1, 8):
            s = slope(p - jnp.concatenate([p[k:], p[:k]], axis=0))
            change = s - jnp.concatenate([s[16 - k :], s[: 16 - k]], axis=0)
            spread = change if spread is None else spread + change
        s = slope(p[:8] - p[8:])
        spread = spread + jnp.concatenate([s, -s], axis=0)
        skill = slope(p - aim[None])
        adjf[:, rows, :] = ccol[rows, :][None] * (skill * (1.0 / M) - 2.0 * KAPPA * spread)
        return carry

    lax.fori_loop(0, 12, score, 0)

    def adj_copy(m, i):
        return pltpu.make_async_remote_copy(
            src_ref=adjsend.at[m, i], dst_ref=adjrecv.at[m, i],
            send_sem=adj_ss.at[m, i], recv_sem=adj_rs.at[m, i],
            device_id=zdev(3 - i), device_id_type=MESH,
        )

    for m in range(4):
        for i in range(3):
            adjsend[m, i] = adjf[4 * i + m].astype(BF16)
            adj_copy(m, i).start()
        adjrecv[m, 3] = adjf[12 + m].astype(BF16)

    def dn_copy(m):
        return pltpu.make_async_remote_copy(
            src_ref=send_dn.at[m], dst_ref=recv_dn.at[m],
            send_sem=dn_ss.at[m], recv_sem=dn_rs.at[m],
            device_id=down, device_id_type=MESH,
        )

    def up_copy(m):
        return pltpu.make_async_remote_copy(
            src_ref=send_up.at[m], dst_ref=recv_up.at[m],
            send_sem=up_ss.at[m], recv_sem=up_rs.at[m],
            device_id=up, device_id_type=MESH,
        )

    outt[...] = jnp.zeros_like(outt)

    def hidden(m):
        for i in range(3):
            adj_copy(m, i).wait_recv()
        adj = jnp.concatenate([adjrecv[m, i] for i in range(4)], axis=1)
        for n in range(4):
            cols = slice(n * 256, n * 256 + 256)
            dact = lax.dot_general(
                adj, wot[:96, cols], (((0,), (0,)), ((), ())), preferred_element_type=F32
            )
            grad = dact * dsil[:, m, :, cols].reshape(512, 256)
            dpre[:, m, :, cols] = grad.astype(BF16).reshape(4, 128, 256)
        outt[:96, :] += jnp.dot(
            adj, act[:, m].reshape(512, 1024), preferred_element_type=F32
        )

    def interpolate(m):
        dp = dpre[:, m].reshape(512, 1024)
        for n in range(4):
            cols = slice(n * 256, n * 256 + 256)
            dinput = jnp.dot(dp, wht[:, cols], preferred_element_type=F32).astype(BF16)
            contrib = jnp.dot(wt[...], dinput, preferred_element_type=F32)
            send_dn[m, :, cols] = contrib[:256].astype(BF16)
            own[m, :, cols] = contrib[256:512]
            send_up[m, :, cols] = contrib[512:].astype(BF16)
        dn_copy(m).start()
        up_copy(m).start()

    def first_half(m, carry):
        hidden(m)
        interpolate(m)
        return carry

    def second_half(m, carry):
        hidden(m)
        return carry

    lax.fori_loop(0, 2, first_half, 0)
    lax.fori_loop(2, 4, second_half, 0)

    turned_out = outt[...].T.reshape(4, 4, 4, 2, 8, 128)
    for c in range(2):
        accf[c, :, :, :, 1024:] = turned_out[:, :, :, c].reshape(4, 4, 32, 128)

    def c_copy(zc):
        return pltpu.make_async_remote_copy(
            src_ref=csend.at[zc], dst_ref=crecv.at[zc],
            send_sem=c_ss.at[zc], recv_sem=c_rs.at[zc],
            device_id=partner, device_id_type=MESH,
        )

    def weights(zc, carry):
        start = pl.multiple_of(zc * 256, 256)
        lhs = xv[:, :, :, pl.ds(start, 256)].reshape(2048, 256)
        for n in range(2):
            cols = slice(n * 512, n * 512 + 512)
            part = lax.dot_general(
                lhs, dpre[:, :, :, cols].reshape(2048, 512), (((0,), (0,)), ((), ())),
                preferred_element_type=F32,
            ).reshape(4, 4, 2, 8, 512)
            for c in range(2):
                accf[c, zc, :, :, cols] = part[:, :, c].reshape(4, 32, 512)
        csend[zc] = accf[oc, zc].astype(BF16)
        c_copy(zc).start()
        return carry

    lax.fori_loop(0, 4, weights, 0)

    def combine(zc, carry):
        c_copy(zc).wait_recv()
        total = accf[cc, zc] + crecv[zc].astype(F32)
        accf[cc, zc] = total
        s1a[zc] = total[:, :, :CA].astype(BF16)
        s1b[:, zc] = total[:, :, CA:].astype(BF16)
        return carry

    def remote(src, dst, ss, rs, dev, k):
        return pltpu.make_async_remote_copy(
            src_ref=src, dst_ref=dst, send_sem=ss.at[k - 1], recv_sem=rs.at[k - 1],
            device_id=dev, device_id_type=MESH,
        )

    def a1(k):
        return remote(s1a.at[(z + k) % 4], r1a.at[k - 1], a1_ss, a1_rs, zdev(k), k)

    def b1(k):
        return remote(s1b.at[(yy + k) % 4], r1b.at[k - 1], b1_ss, b1_rs, ydev(k), k)

    def a2(k):
        return remote(s2a.at[(yy + k) % 4], r2a.at[k - 1], a2_ss, a2_rs, ydev(k), k)

    def b2(k):
        return remote(s2b.at[(z + k) % 4], r2b.at[k - 1], b2_ss, b2_rs, zdev(k), k)

    def x3(k):
        return remote(p3.at[(xx + k) % 4], r3.at[k - 1], x_ss, x_rs, xdev(k), k)

    def last(m, carry):
        interpolate(m)

        @pl.when(m == 2)
        def _():
            lax.fori_loop(0, 4, combine, 0)
            for k in (2, 1, 3):
                a1(k).start()
                b1(k).start()

        return carry

    lax.fori_loop(2, 4, last, 0)

    def finish(m, carry):
        dn_copy(m).wait_recv()
        up_copy(m).wait_recv()
        own[m] = own[m] + recv_dn[m].astype(F32) + recv_up[m].astype(F32)
        return carry

    for k in (1, 3, 2):
        a1(k).wait_recv()
    total = accf[cc, z, :, :, :CA]
    for k in range(3):
        total = total + r1a[k].astype(F32)
    p2a[...] = total
    s2a[...] = total.astype(BF16)
    for k in (2, 1, 3):
        a2(k).start()
    for k in (1, 3, 2):
        b1(k).wait_recv()
    total = accf[cc, :, yy, :, CA:]
    for k in range(3):
        total = total + r1b[k].astype(F32)
    p2b[...] = total
    s2b[...] = total.astype(BF16)
    for k in (2, 1, 3):
        b2(k).start()

    lax.fori_loop(0, 2, finish, 0)

    for k in (1, 3, 2):
        a2(k).wait_recv()
    total = p2a[yy]
    for k in range(3):
        total = total + r2a[k].astype(F32)
    p3[:, :, :CA] = total.reshape(4, 8, CA)
    for k in (1, 3, 2):
        b2(k).wait_recv()
    total = p2b[z]
    for k in range(3):
        total = total + r2b[k].astype(F32)
    p3[:, :, CA:] = total.reshape(4, 8, CW - CA)
    for k in (2, 1, 3):
        x3(k).start()
    lax.fori_loop(2, 3, finish, 0)

    for k in (1, 3, 2):
        x3(k).wait_recv()
    total = p3[xx]
    for k in range(3):
        total = total + r3[k]
    gh_ref[...] = total[:, :1024]
    go_ref[...] = total[:, 1024:]

    lax.fori_loop(3, 4, finish, 0)

    for i in range(3):
        pred_copy(i).wait_send()
        for m in range(4):
            adj_copy(m, i).wait_send()
    for m in range(4):
        dn_copy(m).wait_send()
        up_copy(m).wait_send()
        c_copy(m).wait_send()
    for k in (1, 2, 3):
        for f in (a1, b1, a2, b2, x3):
            f(k).wait_send()


def store(gh_ref, go_ref, mesh_ref, gh_out, go_out, mesh_out, sem):
    copies = [pltpu.make_async_copy(mesh_ref.at[m], mesh_out.at[m], sem.at[m]) for m in range(4)]
    for copy in copies:
        copy.start()
    gh_out[...] = gh_ref[...]
    go_out[...] = go_ref[:, :96]
    for copy in copies:
        copy.wait()


def body(
    grid_input, w_hidden, b_hidden, w_out, b_out, target, channel_weight, interp_weight, block_index
):
    V = pltpu.VMEM
    D = pltpu.SemaphoreType.DMA
    any_spec = pl.BlockSpec(memory_space=pl.ANY)
    vmem_spec = pl.BlockSpec(memory_space=pltpu.VMEM)
    scratch = [
        V((4, 4, 128, 1024), BF16), V((1024, 1024), BF16), V((1024, 1024), BF16),
        V((128, 1024), BF16), V((1024, 128), BF16),
        V((4, 3, 128, 128), BF16), V((96, 128), F32),
        V((4, 4, 128, 1024), BF16), V((4, 4, 128, 1024), F32), V((4, 4, 128, 1024), BF16),
        V((768, 512), BF16), V((128, 128), F32), V((128, 128), F32),
        V((4, 4, 96, 128), BF16), V((3, 4, 96, 128), BF16),
        V((16, 96, 128), F32), V((16, 96, 128), F32),
        V((4, 3, 96, 128), BF16), V((4, 4, 96, 128), BF16), V((128, 1024), F32),
        V((4, 256, 1024), BF16), V((4, 256, 1024), BF16),
        V((4, 256, 1024), BF16), V((4, 256, 1024), BF16),
        V((2, 4, 4, 32, CW), F32), V((4, 4, 32, CW), BF16), V((4, 4, 32, CW), BF16),
        V((4, 4, 32, CA), BF16), V((4, 4, 32, CW - CA), BF16),
        V((3, 4, 32, CA), BF16), V((3, 4, 32, CW - CA), BF16),
        V((4, 32, CA), F32), V((4, 32, CW - CA), F32),
        V((4, 32, CA), BF16), V((4, 32, CW - CA), BF16),
        V((3, 32, CA), BF16), V((3, 32, CW - CA), BF16),
        V((4, 8, CW), F32), V((3, 8, CW), F32),
        D((4,)), D((4,)), D((3,)), D((3,)), D((4, 3)), D((4, 3)),
        D((4,)), D((4,)), D((4,)), D((4,)), D((4,)), D((4,)),
        D((3,)), D((3,)), D((3,)), D((3,)), D((3,)), D((3,)), D((3,)), D((3,)),
        D((3,)), D((3,)),
    ]
    held = pl.pallas_call(
        kernel,
        out_shape=(V((8, 1024), F32), V((8, 128), F32), V((4, 256, 1024), F32)),
        in_specs=[any_spec] * 3 + [vmem_spec] * 3 + [any_spec] * 2
        + [pl.BlockSpec(memory_space=pltpu.SMEM)],
        out_specs=(vmem_spec, vmem_spec, vmem_spec),
        scratch_shapes=scratch,
        compiler_params=pltpu.CompilerParams(
            collective_id=0, has_side_effects=True, vmem_limit_bytes=54 * 2**20
        ),
    )(
        grid_input, w_hidden, w_out.T, b_hidden[None], b_out[None], channel_weight[None],
        target, interp_weight, block_index,
    )
    held = [pltpu.with_memory_space_constraint(h, pltpu.VMEM) for h in held]
    return pl.pallas_call(
        store,
        out_shape=(
            jax.ShapeDtypeStruct((8, 1024), F32),
            jax.ShapeDtypeStruct((8, 96), F32),
            jax.ShapeDtypeStruct((4, 256, 1024), F32),
        ),
        in_specs=[vmem_spec] * 3,
        out_specs=(vmem_spec, vmem_spec, any_spec),
        scratch_shapes=[D((4,))],
        compiler_params=pltpu.CompilerParams(vmem_limit_bytes=2**20),
    )(*held)


def solution(mesh):
    placed = (
        P("member", "region", None),
        P(),
        P(),
        P(),
        P(),
        P(None, "region"),
        P(),
        P("region", None, None, None),
        P("region", None),
    )
    return jax.shard_map(
        body,
        mesh=mesh,
        in_specs=placed,
        out_specs=(
            P(("member", "region"), None),
            P(("member", "region"), None),
            P("member", "region", None),
        ),
        check_vma=False,
    )
```

```python
import jax
import jax.numpy as jnp
from jax import lax
from jax.experimental import pallas as pl
from jax.experimental.pallas import tpu as pltpu
from jax.sharding import PartitionSpec as P

MESH = pl.DeviceIdType.MESH
F32 = jnp.float32
BF16 = jnp.bfloat16
M = 16
ALPHA = 0.95
SMOOTH = 0.25
KAPPA = ALPHA / (2.0 * M * (M - 1)) + (1.0 - ALPHA) / (2.0 * M * M)
CA = 640
CW = 1152


def kernel(
    x_hbm, wh_hbm, wot_hbm, bh_ref, bo_ref, cw_ref, tgt_hbm, tile_hbm, bi_ref,
    gh_ref, go_ref, own,
    xv, wh, wht, wot, tiles, tgt, act, dsil, dpre, wt, bcol, ccol,
    predsend, predrecv, pf, adjf, adjsend, adjrecv, outt,
    send_dn, send_up, recv_dn, recv_up,
    accf, csend, crecv, s1a, s1b, ra, rb, p2a, p2b, s2a, s2b, r2a, r2b, p3, r3,
    load_sem, x_sem, pred_ss, pred_rs, adj_ss, adj_rs, dn_ss, dn_rs, up_ss, up_rs,
    c_ss, c_rs, a1_ss, a1_rs, b1_ss, b1_rs, a2_ss, a2_rs, b2_ss, b2_rs, x_ss, x_rs,
):
    z = lax.axis_index("member")
    r = lax.axis_index("region")
    yy, xx, cc = r // 8, (r // 2) % 4, r % 2
    oc = 1 - cc

    def zdev(k):
        return ((z + k) % 4, r)

    def ydev(k):
        return (z, ((yy + k) % 4) * 8 + xx * 2 + cc)

    def xdev(k):
        return (z, yy * 8 + ((xx + k) % 4) * 2 + cc)

    partner = (z, r + 1 - 2 * cc)
    up = (z, (r + 1) % 32)
    down = (z, (r + 31) % 32)

    def block_of(i):
        return (z + 1 + i) % 4

    barrier = pltpu.get_barrier_semaphore()
    peers = [f(k) for f in (zdev, ydev, xdev) for k in (1, 2, 3)] + [up, down]
    for peer in peers:
        pl.semaphore_signal(barrier, inc=1, device_id=peer, device_id_type=MESH)

    load_wh = pltpu.make_async_copy(wh_hbm, wh, load_sem.at[0])
    load_wh.start()

    def x_copy(i):
        start = pl.multiple_of(block_of(i) * 128, 128)
        return pltpu.make_async_copy(
            x_hbm.at[:, pl.ds(start, 128), :], xv.at[i], x_sem.at[i]
        )

    x_copy(0).start()
    load_wot = pltpu.make_async_copy(wot_hbm, wot, load_sem.at[1])
    load_wot.start()
    for i in range(1, 4):
        x_copy(i).start()
    load_tiles = pltpu.make_async_copy(tile_hbm, tiles, load_sem.at[2])
    load_tiles.start()
    load_tgt = pltpu.make_async_copy(
        tgt_hbm.at[:, pl.ds(pl.multiple_of(z * 128, 128), 128)], tgt, load_sem.at[3]
    )
    load_tgt.start()

    def pred_copy(i):
        return pltpu.make_async_remote_copy(
            src_ref=predsend.at[i], dst_ref=predrecv.at[i],
            send_sem=pred_ss.at[i], recv_sem=pred_rs.at[i],
            device_id=zdev(i + 1), device_id_type=MESH,
        )

    load_wot.wait()
    load_wh.wait()

    def forward(i, carry):
        x_copy(i).wait()
        xb = xv[i].reshape(512, 1024)
        for n in range(4):
            cols = slice(n * 256, n * 256 + 256)
            pre = jnp.dot(xb, wh[:, cols], preferred_element_type=F32) + bh_ref[:, cols]
            sig = 0.5 + 0.5 * jnp.tanh(0.5 * pre)
            silu = pre * sig
            act[i, :, :, cols] = silu.astype(BF16).reshape(4, 128, 256)
            dsil[i, :, :, cols] = (sig + silu * (1.0 - sig)).reshape(4, 128, 256)
        predt = lax.dot_general(
            wot[...], act[i].reshape(512, 1024), (((1,), (1,)), ((), ())),
            preferred_element_type=F32,
        ).astype(BF16)
        for m in range(4):
            predsend[i, m] = predt[:, m * 128 : m * 128 + 128]

        @pl.when(i == 0)
        def _():
            pl.semaphore_wait(barrier, len(peers))

        @pl.when(i < 3)
        def _():
            pred_copy(i).start()

        return carry

    lax.fori_loop(0, 4, forward, 0)

    load_tiles.wait()

    def build(i, carry):
        b = block_of(i)
        place = pl.ds(pl.multiple_of(i * 128, 128), 128)
        slots = []
        turned = []
        for k in range(3):
            index = bi_ref[b, k]
            relative = (index // 2 - r + 33) % 32
            slots.append(relative * 2 + index % 2)
            turned.append(tiles[b, k].astype(F32).T)
        for s in range(6):
            total = None
            for k in range(3):
                term = turned[k] * jnp.where(slots[k] == s, 1.0, 0.0)
                total = term if total is None else total + term
            wt[s * 128 : s * 128 + 128, place] = total.astype(BF16)
        return carry

    lax.fori_loop(0, 4, build, 0)

    for n in range(4):
        wht[:, n * 256 : n * 256 + 256] = wh[n * 256 : n * 256 + 256, :].T

    bcol[...] = jnp.zeros_like(bcol)
    ccol[...] = jnp.zeros_like(ccol)
    bcol[:, :96] = jnp.broadcast_to(bo_ref[...], (128, 96))
    ccol[:, :96] = jnp.broadcast_to(cw_ref[...], (128, 96))
    bcol[...] = bcol[...].T
    ccol[...] = ccol[...].T
    load_tgt.wait()

    pf[12:16] = predsend[3].astype(F32)
    for i in range(3):
        pred_copy(i).wait_recv()
        pf[4 * i : 4 * i + 4] = predrecv[i].astype(F32)

    def score(t, carry):
        rows = pl.ds(pl.multiple_of(t * 8, 8), 8)
        p = pf[:, rows, :]
        aim = tgt[rows, :] - bcol[rows, :]

        def slope(d):
            return d * lax.rsqrt(d * d + SMOOTH * SMOOTH)

        spread = None
        for k in range(1, 8):
            s = slope(p - jnp.concatenate([p[k:], p[:k]], axis=0))
            change = s - jnp.concatenate([s[16 - k :], s[: 16 - k]], axis=0)
            spread = change if spread is None else spread + change
        s = slope(p[:8] - p[8:])
        spread = spread + jnp.concatenate([s, -s], axis=0)
        skill = slope(p - aim[None])
        adjf[:, rows, :] = ccol[rows, :][None] * (skill * (1.0 / M) - 2.0 * KAPPA * spread)
        return carry

    lax.fori_loop(0, 12, score, 0)

    def adj_copy(m, i):
        return pltpu.make_async_remote_copy(
            src_ref=adjsend.at[m, i], dst_ref=adjrecv.at[m, i],
            send_sem=adj_ss.at[m, i], recv_sem=adj_rs.at[m, i],
            device_id=zdev(3 - i), device_id_type=MESH,
        )

    for m in range(4):
        for i in range(3):
            adjsend[m, i] = adjf[4 * i + m].astype(BF16)
            adj_copy(m, i).start()
        adjrecv[m, 3] = adjf[12 + m].astype(BF16)

    def dn_copy(m):
        return pltpu.make_async_remote_copy(
            src_ref=send_dn.at[m], dst_ref=recv_dn.at[m],
            send_sem=dn_ss.at[m], recv_sem=dn_rs.at[m],
            device_id=down, device_id_type=MESH,
        )

    def up_copy(m):
        return pltpu.make_async_remote_copy(
            src_ref=send_up.at[m], dst_ref=recv_up.at[m],
            send_sem=up_ss.at[m], recv_sem=up_rs.at[m],
            device_id=up, device_id_type=MESH,
        )

    outt[...] = jnp.zeros_like(outt)

    def hidden(m):
        for i in range(3):
            adj_copy(m, i).wait_recv()
        adj = jnp.concatenate([adjrecv[m, i] for i in range(4)], axis=1)
        for n in range(4):
            cols = slice(n * 256, n * 256 + 256)
            dact = lax.dot_general(
                adj, wot[:, cols], (((0,), (0,)), ((), ())), preferred_element_type=F32
            )
            grad = dact * dsil[:, m, :, cols].reshape(512, 256)
            dpre[:, m, :, cols] = grad.astype(BF16).reshape(4, 128, 256)
        outt[:96, :] += jnp.dot(
            adj, act[:, m].reshape(512, 1024), preferred_element_type=F32
        )

    def interpolate(m):
        dp = dpre[:, m].reshape(512, 1024)
        dinput = jnp.dot(dp, wht[...], preferred_element_type=F32).astype(BF16)
        contrib = jnp.dot(wt[...], dinput, preferred_element_type=F32)
        send_dn[m] = contrib[:256].astype(BF16)
        own[m] = contrib[256:512]
        send_up[m] = contrib[512:].astype(BF16)
        dn_copy(m).start()
        up_copy(m).start()

    def first_half(m, carry):
        hidden(m)
        interpolate(m)
        return carry

    def second_half(m, carry):
        hidden(m)
        return carry

    lax.fori_loop(0, 2, first_half, 0)
    lax.fori_loop(2, 4, second_half, 0)

    turned_out = outt[...].T.reshape(4, 4, 4, 2, 8, 128)
    for c in range(2):
        accf[c, :, :, :, 1024:] = turned_out[:, :, :, c].reshape(4, 4, 32, 128)

    def c_copy(zc):
        return pltpu.make_async_remote_copy(
            src_ref=csend.at[zc], dst_ref=crecv.at[zc],
            send_sem=c_ss.at[zc], recv_sem=c_rs.at[zc],
            device_id=partner, device_id_type=MESH,
        )

    def weights(zc, carry):
        start = pl.multiple_of(zc * 256, 256)
        lhs = xv[:, :, :, pl.ds(start, 256)].reshape(2048, 256)
        for n in range(2):
            cols = slice(n * 512, n * 512 + 512)
            part = lax.dot_general(
                lhs, dpre[:, :, :, cols].reshape(2048, 512), (((0,), (0,)), ((), ())),
                preferred_element_type=F32,
            ).reshape(4, 4, 2, 8, 512)
            for c in range(2):
                accf[c, zc, :, :, cols] = part[:, :, c].reshape(4, 32, 512)
        csend[zc] = accf[oc, zc].astype(BF16)
        c_copy(zc).start()
        return carry

    lax.fori_loop(0, 4, weights, 0)

    def combine(zc, carry):
        c_copy(zc).wait_recv()
        total = accf[cc, zc] + crecv[zc].astype(F32)
        accf[cc, zc] = total
        s1a[zc] = total[:, :, :CA].astype(BF16)
        s1b[:, zc] = total[:, :, CA:].astype(BF16)
        return carry

    def remote(src, dst, ss, rs, dev, k):
        return pltpu.make_async_remote_copy(
            src_ref=src, dst_ref=dst, send_sem=ss.at[k - 1], recv_sem=rs.at[k - 1],
            device_id=dev, device_id_type=MESH,
        )

    def ring(dev, me, s1, relay, direct, onward, summed, get, ss, rs):
        after, before, far = (me + 1) % 4, (me + 3) % 4, (me + 2) % 4
        low, high = slice(0, 2), slice(2, 4)

        def copy(n):
            src, dst, k = (
                (s1.at[far, low], relay.at[0], 1),
                (s1.at[far, high], relay.at[1], 3),
                (s1.at[after, high], direct.at[0], 1),
                (s1.at[before, low], direct.at[1], 3),
                (onward.at[0], summed.at[0], 1),
                (onward.at[1], summed.at[1], 3),
            )[n]
            return pltpu.make_async_remote_copy(
                src_ref=src, dst_ref=dst, send_sem=ss.at[n], recv_sem=rs.at[n],
                device_id=dev(k), device_id_type=MESH,
            )

        def begin():
            for n in range(4):
                copy(n).start()

        def pass_on():
            copy(0).wait_recv()
            onward[0] = (get(after, low) + relay[0].astype(F32)).astype(BF16)
            copy(4).start()
            copy(1).wait_recv()
            onward[1] = (get(before, high) + relay[1].astype(F32)).astype(BF16)
            copy(5).start()

        def end(out, out16):
            for n in range(2, 6):
                copy(n).wait_recv()
            first = get(me, low) + summed[0].astype(F32) + direct[1].astype(F32)
            second = get(me, high) + summed[1].astype(F32) + direct[0].astype(F32)
            out[0:2] = first
            out[2:4] = second
            out16[0:2] = first.astype(BF16)
            out16[2:4] = second.astype(BF16)

        def sent():
            for n in range(6):
                copy(n).wait_send()

        return begin, pass_on, end, sent

    ring_a = ring(
        zdev, z, s1a, ra.at[0], ra.at[1], ra.at[2], ra.at[3],
        lambda j, part: accf[cc, j, part, :, :CA], a1_ss, a1_rs,
    )
    ring_b = ring(
        ydev, yy, s1b, rb.at[0], rb.at[1], rb.at[2], rb.at[3],
        lambda j, part: accf[cc, part, j, :, CA:], b1_ss, b1_rs,
    )

    def a2(k):
        return remote(s2a.at[(yy + k) % 4], r2a.at[k - 1], a2_ss, a2_rs, ydev(k), k)

    def b2(k):
        return remote(s2b.at[(z + k) % 4], r2b.at[k - 1], b2_ss, b2_rs, zdev(k), k)

    def x3(k):
        return remote(p3.at[(xx + k) % 4], r3.at[k - 1], x_ss, x_rs, xdev(k), k)

    def last(m, carry):
        interpolate(m)

        @pl.when(m == 2)
        def _():
            lax.fori_loop(0, 4, combine, 0)
            ring_a[0]()
            ring_b[0]()

        return carry

    lax.fori_loop(2, 4, last, 0)

    def finish(m, carry):
        dn_copy(m).wait_recv()
        up_copy(m).wait_recv()
        own[m] = own[m] + recv_dn[m].astype(F32) + recv_up[m].astype(F32)
        return carry

    ring_a[1]()
    ring_b[1]()
    lax.fori_loop(0, 1, finish, 0)
    ring_a[2](p2a, s2a)
    for k in (2, 1, 3):
        a2(k).start()
    ring_b[2](p2b, s2b)
    for k in (2, 1, 3):
        b2(k).start()

    lax.fori_loop(1, 2, finish, 0)

    for k in (1, 3, 2):
        a2(k).wait_recv()
    total = p2a[yy]
    for k in range(3):
        total = total + r2a[k].astype(F32)
    p3[:, :, :CA] = total.reshape(4, 8, CA)
    for k in (1, 3, 2):
        b2(k).wait_recv()
    total = p2b[z]
    for k in range(3):
        total = total + r2b[k].astype(F32)
    p3[:, :, CA:] = total.reshape(4, 8, CW - CA)
    for k in (2, 1, 3):
        x3(k).start()
    lax.fori_loop(2, 3, finish, 0)

    for k in (1, 3, 2):
        x3(k).wait_recv()
    total = p3[xx]
    for k in range(3):
        total = total + r3[k]
    gh_ref[...] = total[:, :1024]
    go_ref[...] = total[:, 1024:]

    lax.fori_loop(3, 4, finish, 0)

    for i in range(3):
        pred_copy(i).wait_send()
        for m in range(4):
            adj_copy(m, i).wait_send()
    for m in range(4):
        dn_copy(m).wait_send()
        up_copy(m).wait_send()
        c_copy(m).wait_send()
    for k in (1, 2, 3):
        for f in (a2, b2, x3):
            f(k).wait_send()
    ring_a[3]()
    ring_b[3]()


def store(gh_ref, go_ref, mesh_ref, gh_out, go_out, mesh_out, sem):
    copies = [pltpu.make_async_copy(mesh_ref.at[m], mesh_out.at[m], sem.at[m]) for m in range(4)]
    for copy in copies:
        copy.start()
    gh_out[...] = gh_ref[...]
    go_out[...] = go_ref[:, :96]
    for copy in copies:
        copy.wait()


def body(
    grid_input, w_hidden, b_hidden, w_out, b_out, target, channel_weight, interp_weight, block_index
):
    V = pltpu.VMEM
    D = pltpu.SemaphoreType.DMA
    any_spec = pl.BlockSpec(memory_space=pl.ANY)
    vmem_spec = pl.BlockSpec(memory_space=pltpu.VMEM)
    scratch = [
        V((4, 4, 128, 1024), BF16), V((1024, 1024), BF16), V((1024, 1024), BF16),
        V((96, 1024), BF16),
        V((4, 3, 128, 128), BF16), V((96, 128), F32),
        V((4, 4, 128, 1024), BF16), V((4, 4, 128, 1024), F32), V((4, 4, 128, 1024), BF16),
        V((768, 512), BF16), V((128, 128), F32), V((128, 128), F32),
        V((4, 4, 96, 128), BF16), V((3, 4, 96, 128), BF16),
        V((16, 96, 128), F32), V((16, 96, 128), F32),
        V((4, 3, 96, 128), BF16), V((4, 4, 96, 128), BF16), V((128, 1024), F32),
        V((4, 256, 1024), BF16), V((4, 256, 1024), BF16),
        V((4, 256, 1024), BF16), V((4, 256, 1024), BF16),
        V((2, 4, 4, 32, CW), F32), V((4, 4, 32, CW), BF16), V((4, 4, 32, CW), BF16),
        V((4, 4, 32, CA), BF16), V((4, 4, 32, CW - CA), BF16),
        V((4, 2, 2, 32, CA), BF16), V((4, 2, 2, 32, CW - CA), BF16),
        V((4, 32, CA), F32), V((4, 32, CW - CA), F32),
        V((4, 32, CA), BF16), V((4, 32, CW - CA), BF16),
        V((3, 32, CA), BF16), V((3, 32, CW - CA), BF16),
        V((4, 8, CW), F32), V((3, 8, CW), F32),
        D((4,)), D((4,)), D((3,)), D((3,)), D((4, 3)), D((4, 3)),
        D((4,)), D((4,)), D((4,)), D((4,)), D((4,)), D((4,)),
        D((6,)), D((6,)), D((6,)), D((6,)), D((3,)), D((3,)), D((3,)), D((3,)),
        D((3,)), D((3,)),
    ]
    held = pl.pallas_call(
        kernel,
        out_shape=(V((8, 1024), F32), V((8, 128), F32), V((4, 256, 1024), F32)),
        in_specs=[any_spec] * 3 + [vmem_spec] * 3 + [any_spec] * 2
        + [pl.BlockSpec(memory_space=pltpu.SMEM)],
        out_specs=(vmem_spec, vmem_spec, vmem_spec),
        scratch_shapes=scratch,
        compiler_params=pltpu.CompilerParams(
            collective_id=0, has_side_effects=True, vmem_limit_bytes=54 * 2**20
        ),
    )(
        grid_input, w_hidden, w_out.T, b_hidden[None], b_out[None], channel_weight[None],
        target, interp_weight, block_index,
    )
    held = [pltpu.with_memory_space_constraint(h, pltpu.VMEM) for h in held]
    return pl.pallas_call(
        store,
        out_shape=(
            jax.ShapeDtypeStruct((8, 1024), F32),
            jax.ShapeDtypeStruct((8, 96), F32),
            jax.ShapeDtypeStruct((4, 256, 1024), F32),
        ),
        in_specs=[vmem_spec] * 3,
        out_specs=(vmem_spec, vmem_spec, any_spec),
        scratch_shapes=[D((4,))],
        compiler_params=pltpu.CompilerParams(vmem_limit_bytes=2**20),
    )(*held)


def solution(mesh):
    placed = (
        P("member", "region", None),
        P(),
        P(),
        P(),
        P(),
        P(None, "region"),
        P(),
        P("region", None, None, None),
        P("region", None),
    )
    return jax.shard_map(
        body,
        mesh=mesh,
        in_specs=placed,
        out_specs=(
            P(("member", "region"), None),
            P(("member", "region"), None),
            P("member", "region", None),
        ),
        check_vma=False,
    )
```

```python
import jax
import jax.numpy as jnp
from jax import lax
from jax.experimental import pallas as pl
from jax.experimental.pallas import tpu as pltpu
from jax.sharding import PartitionSpec as P

MESH = pl.DeviceIdType.MESH
F32 = jnp.float32
BF16 = jnp.bfloat16
M = 16
ALPHA = 0.95
SMOOTH = 0.25
KAPPA = ALPHA / (2.0 * M * (M - 1)) + (1.0 - ALPHA) / (2.0 * M * M)
CW = 1152


def kernel(
    x_hbm, wh_hbm, wot_hbm, bh_ref, bo_ref, cw_ref, tgt_hbm, tile_hbm, bi_ref,
    gh_ref, go_ref, own,
    xv, wh, wht, wot, tiles, tgt, act, dsil, dpre, wt, bcol, ccol,
    predsend, predrecv, pf, adjf, adjsend, adjrecv, outt,
    send_dn, send_up, recv_dn, recv_up,
    accf, csend, crecv, s1, ring_in, onward, p2, s2, r2, p3, r3,
    load_sem, x_sem, pred_ss, pred_rs, adj_ss, adj_rs, dn_ss, dn_rs, up_ss, up_rs,
    c_ss, c_rs, ring_ss, ring_rs, y_ss, y_rs, x_ss, x_rs,
):
    z = lax.axis_index("member")
    r = lax.axis_index("region")
    yy, xx, cc = r // 8, (r // 2) % 4, r % 2
    oc = 1 - cc

    def zdev(k):
        return ((z + k) % 4, r)

    def ydev(k):
        return (z, ((yy + k) % 4) * 8 + xx * 2 + cc)

    def xdev(k):
        return (z, yy * 8 + ((xx + k) % 4) * 2 + cc)

    partner = (z, r + 1 - 2 * cc)
    up = (z, (r + 1) % 32)
    down = (z, (r + 31) % 32)

    def block_of(i):
        return (z + 1 + i) % 4

    barrier = pltpu.get_barrier_semaphore()
    peers = [f(k) for f in (zdev, ydev, xdev) for k in (1, 2, 3)] + [up, down]
    for peer in peers:
        pl.semaphore_signal(barrier, inc=1, device_id=peer, device_id_type=MESH)

    load_wh = pltpu.make_async_copy(wh_hbm, wh, load_sem.at[0])
    load_wh.start()

    def x_copy(i):
        start = pl.multiple_of(block_of(i) * 128, 128)
        return pltpu.make_async_copy(
            x_hbm.at[:, pl.ds(start, 128), :], xv.at[i], x_sem.at[i]
        )

    x_copy(0).start()
    load_wot = pltpu.make_async_copy(wot_hbm, wot, load_sem.at[1])
    load_wot.start()
    for i in range(1, 4):
        x_copy(i).start()
    load_tiles = pltpu.make_async_copy(tile_hbm, tiles, load_sem.at[2])
    load_tiles.start()
    load_tgt = pltpu.make_async_copy(
        tgt_hbm.at[:, pl.ds(pl.multiple_of(z * 128, 128), 128)], tgt, load_sem.at[3]
    )
    load_tgt.start()

    def pred_copy(i):
        return pltpu.make_async_remote_copy(
            src_ref=predsend.at[i], dst_ref=predrecv.at[i],
            send_sem=pred_ss.at[i], recv_sem=pred_rs.at[i],
            device_id=zdev(i + 1), device_id_type=MESH,
        )

    load_wot.wait()
    load_wh.wait()

    def forward(i, carry):
        x_copy(i).wait()
        xb = xv[i].reshape(512, 1024)
        for n in range(4):
            cols = slice(n * 256, n * 256 + 256)
            pre = jnp.dot(xb, wh[:, cols], preferred_element_type=F32) + bh_ref[:, cols]
            sig = 0.5 + 0.5 * jnp.tanh(0.5 * pre)
            silu = pre * sig
            act[i, :, :, cols] = silu.astype(BF16).reshape(4, 128, 256)
            dsil[i, :, :, cols] = (sig + silu * (1.0 - sig)).reshape(4, 128, 256)
        predt = lax.dot_general(
            wot[...], act[i].reshape(512, 1024), (((1,), (1,)), ((), ())),
            preferred_element_type=F32,
        ).astype(BF16)
        for m in range(4):
            predsend[i, m] = predt[:, m * 128 : m * 128 + 128]

        @pl.when(i == 1)
        def _():
            pl.semaphore_wait(barrier, len(peers))
            pred_copy(0).start()
            pred_copy(1).start()

        @pl.when(i == 2)
        def _():
            pred_copy(2).start()

        return carry

    lax.fori_loop(0, 4, forward, 0)

    load_tiles.wait()

    def build(i, carry):
        b = block_of(i)
        place = pl.ds(pl.multiple_of(i * 128, 128), 128)
        slots = []
        turned = []
        for k in range(3):
            index = bi_ref[b, k]
            relative = (index // 2 - r + 33) % 32
            slots.append(relative * 2 + index % 2)
            turned.append(tiles[b, k].astype(F32).T)
        for s in range(6):
            total = None
            for k in range(3):
                term = turned[k] * jnp.where(slots[k] == s, 1.0, 0.0)
                total = term if total is None else total + term
            wt[s * 128 : s * 128 + 128, place] = total.astype(BF16)
        return carry

    lax.fori_loop(0, 4, build, 0)

    bcol[...] = jnp.zeros_like(bcol)
    ccol[...] = jnp.zeros_like(ccol)
    bcol[:, :96] = jnp.broadcast_to(bo_ref[...], (128, 96))
    ccol[:, :96] = jnp.broadcast_to(cw_ref[...], (128, 96))
    bcol[...] = bcol[...].T
    ccol[...] = ccol[...].T
    load_tgt.wait()

    pf[12:16] = predsend[3].astype(F32)
    for i in range(3):
        pred_copy(i).wait_recv()
        pf[4 * i : 4 * i + 4] = predrecv[i].astype(F32)

    def score(t, carry):
        rows = pl.ds(pl.multiple_of(t * 8, 8), 8)
        p = pf[:, rows, :]
        aim = tgt[rows, :] - bcol[rows, :]

        def slope(d):
            return d * lax.rsqrt(d * d + SMOOTH * SMOOTH)

        spread = None
        for k in range(1, 8):
            s = slope(p - jnp.concatenate([p[k:], p[:k]], axis=0))
            change = s - jnp.concatenate([s[16 - k :], s[: 16 - k]], axis=0)
            spread = change if spread is None else spread + change
        s = slope(p[:8] - p[8:])
        spread = spread + jnp.concatenate([s, -s], axis=0)
        skill = slope(p - aim[None])
        adjf[:, rows, :] = ccol[rows, :][None] * (skill * (1.0 / M) - 2.0 * KAPPA * spread)
        return carry

    lax.fori_loop(0, 12, score, 0)

    def adj_copy(m, i):
        return pltpu.make_async_remote_copy(
            src_ref=adjsend.at[m, i], dst_ref=adjrecv.at[m, i],
            send_sem=adj_ss.at[m, i], recv_sem=adj_rs.at[m, i],
            device_id=zdev(3 - i), device_id_type=MESH,
        )

    for m in range(4):
        for i in range(3):
            adjsend[m, i] = adjf[4 * i + m].astype(BF16)
            adj_copy(m, i).start()
        adjrecv[m, 3] = adjf[12 + m].astype(BF16)

    def dn_copy(m, h):
        return pltpu.make_async_remote_copy(
            src_ref=send_dn.at[m, h], dst_ref=recv_dn.at[m, h],
            send_sem=dn_ss.at[m, h], recv_sem=dn_rs.at[m, h],
            device_id=down, device_id_type=MESH,
        )

    def up_copy(m, h):
        return pltpu.make_async_remote_copy(
            src_ref=send_up.at[m, h], dst_ref=recv_up.at[m, h],
            send_sem=up_ss.at[m, h], recv_sem=up_rs.at[m, h],
            device_id=up, device_id_type=MESH,
        )

    outt[...] = jnp.zeros_like(outt)
    for n in range(4):
        wht[:, n * 256 : n * 256 + 256] = wh[n * 256 : n * 256 + 256, :].T

    def hidden(m):
        for i in range(3):
            adj_copy(m, i).wait_recv()
        adj = jnp.concatenate([adjrecv[m, i] for i in range(4)], axis=1)
        for n in range(4):
            cols = slice(n * 256, n * 256 + 256)
            dact = lax.dot_general(
                adj, wot[:, cols], (((0,), (0,)), ((), ())), preferred_element_type=F32
            )
            grad = dact * dsil[:, m, :, cols].reshape(512, 256)
            dpre[:, m, :, cols] = grad.astype(BF16).reshape(4, 128, 256)
        outt[:96, :] += jnp.dot(
            adj, act[:, m].reshape(512, 1024), preferred_element_type=F32
        )

    def interpolate(m):
        dp = dpre[:, m].reshape(512, 1024)
        for h in range(2):
            cols = slice(h * 512, h * 512 + 512)
            dinput = jnp.dot(dp, wht[:, cols], preferred_element_type=F32).astype(BF16)
            contrib = jnp.dot(wt[...], dinput, preferred_element_type=F32)
            send_dn[m, h] = contrib[:256].astype(BF16)
            own[m, :, cols] = contrib[256:512]
            send_up[m, h] = contrib[512:].astype(BF16)
            if h == 0:
                dn_copy(m, h).start()
                up_copy(m, h).start()
            else:

                @pl.when(m < 3)
                def _():
                    dn_copy(m, 1).start()
                    up_copy(m, 1).start()

    def first_half(m, carry):
        hidden(m)
        interpolate(m)
        return carry

    def second_half(m, carry):
        hidden(m)
        return carry

    lax.fori_loop(0, 2, first_half, 0)
    lax.fori_loop(2, 4, second_half, 0)

    turned_out = outt[...].T.reshape(4, 4, 4, 2, 8, 128)
    for c in range(2):
        accf[c, :, :, :, 1024:] = turned_out[:, :, :, c].reshape(4, 4, 32, 128)

    def row_of(j):
        return (z + 2 + j + (j // 2) * (2 * j - 3)) % 4

    def c_copy(j):
        return pltpu.make_async_remote_copy(
            src_ref=csend.at[j], dst_ref=crecv.at[j],
            send_sem=c_ss.at[j], recv_sem=c_rs.at[j],
            device_id=partner, device_id_type=MESH,
        )

    def gradient(j):
        zc = row_of(j)
        start = pl.multiple_of(zc * 256, 256)
        lhs = xv[:, :, :, pl.ds(start, 256)].reshape(2048, 256)
        for n in range(2):
            cols = slice(n * 512, n * 512 + 512)
            part = lax.dot_general(
                lhs, dpre[:, :, :, cols].reshape(2048, 512), (((0,), (0,)), ((), ())),
                preferred_element_type=F32,
            ).reshape(4, 4, 2, 8, 512)
            for c in range(2):
                accf[c, zc, :, :, cols] = part[:, :, c].reshape(4, 32, 512)
        csend[j] = accf[oc, zc].astype(BF16)
        c_copy(j).start()

    def combine(j):
        zc = row_of(j)
        c_copy(j).wait_recv()
        total = accf[cc, zc] + crecv[j].astype(F32)
        accf[cc, zc] = total
        s1[zc] = total.astype(BF16)

    def remote(src, dst, ss, rs, dev, k):
        return pltpu.make_async_remote_copy(
            src_ref=src, dst_ref=dst, send_sem=ss.at[k - 1], recv_sem=rs.at[k - 1],
            device_id=dev, device_id_type=MESH,
        )

    after, before, far = (z + 1) % 4, (z + 3) % 4, (z + 2) % 4
    low, high = slice(0, 2), slice(2, 4)

    def ring(n):
        src, dst, k = (
            (s1.at[far, low], ring_in.at[0], 1),
            (s1.at[far, high], ring_in.at[1], 3),
            (s1.at[after, high], ring_in.at[2], 1),
            (s1.at[before, low], ring_in.at[3], 3),
            (onward.at[0], ring_in.at[4], 1),
            (onward.at[1], ring_in.at[5], 3),
        )[n]
        return pltpu.make_async_remote_copy(
            src_ref=src, dst_ref=dst, send_sem=ring_ss.at[n], recv_sem=ring_rs.at[n],
            device_id=zdev(k), device_id_type=MESH,
        )

    def y2(k):
        return remote(s2.at[(yy + k) % 4], r2.at[k - 1], y_ss, y_rs, ydev(k), k)

    def x3(k):
        return remote(p3.at[(xx + k) % 4], r3.at[k - 1], x_ss, x_rs, xdev(k), k)

    def weights(j, carry):
        gradient(j)

        @pl.when(j == 2)
        def _():
            combine(0)
            ring(0).start()
            ring(1).start()

        @pl.when(j == 3)
        def _():
            combine(1)
            ring(3).start()

        return carry

    lax.fori_loop(0, 4, weights, 0)

    def pass_on():
        ring(0).wait_recv()
        onward[0] = (accf[cc, after, low] + ring_in[0].astype(F32)).astype(BF16)
        ring(4).start()
        ring(1).wait_recv()
        onward[1] = (accf[cc, before, high] + ring_in[1].astype(F32)).astype(BF16)
        ring(5).start()

    combine(2)
    ring(2).start()

    def last(m, carry):
        interpolate(m)

        @pl.when(m == 2)
        def _():
            combine(3)
            pass_on()

        return carry

    lax.fori_loop(2, 4, last, 0)

    def finish(m, carry):
        for h in range(2):
            cols = slice(h * 512, h * 512 + 512)
            dn_copy(m, h).wait_recv()
            up_copy(m, h).wait_recv()
            own[m, :, cols] = (
                own[m, :, cols] + recv_dn[m, h].astype(F32) + recv_up[m, h].astype(F32)
            )
        return carry

    lax.fori_loop(0, 1, finish, 0)
    for n in range(2, 6):
        ring(n).wait_recv()
    first = accf[cc, z, low] + ring_in[4].astype(F32) + ring_in[3].astype(F32)
    second = accf[cc, z, high] + ring_in[5].astype(F32) + ring_in[2].astype(F32)
    p2[0:2] = first
    p2[2:4] = second
    s2[0:2] = first.astype(BF16)
    s2[2:4] = second.astype(BF16)
    for k in (2, 1, 3):
        y2(k).start()

    lax.fori_loop(1, 2, finish, 0)

    for k in (1, 3, 2):
        y2(k).wait_recv()
    total = p2[yy]
    for k in range(3):
        total = total + r2[k].astype(F32)
    p3[...] = total.reshape(4, 8, CW)
    for k in (2, 1, 3):
        x3(k).start()
    dn_copy(3, 1).start()
    up_copy(3, 1).start()
    lax.fori_loop(2, 3, finish, 0)

    for k in (1, 3, 2):
        x3(k).wait_recv()
    total = p3[xx]
    for k in range(3):
        total = total + r3[k]
    gh_ref[...] = total[:, :1024]
    go_ref[...] = total[:, 1024:]

    lax.fori_loop(3, 4, finish, 0)

    for i in range(3):
        pred_copy(i).wait_send()
        for m in range(4):
            adj_copy(m, i).wait_send()
    for m in range(4):
        for h in range(2):
            dn_copy(m, h).wait_send()
            up_copy(m, h).wait_send()
        c_copy(m).wait_send()
    for k in (1, 2, 3):
        for f in (y2, x3):
            f(k).wait_send()
    for n in range(6):
        ring(n).wait_send()


def store(gh_ref, go_ref, mesh_ref, gh_out, go_out, mesh_out, sem):
    copies = [pltpu.make_async_copy(mesh_ref.at[m], mesh_out.at[m], sem.at[m]) for m in range(4)]
    for copy in copies:
        copy.start()
    gh_out[...] = gh_ref[...]
    go_out[...] = go_ref[:, :96]
    for copy in copies:
        copy.wait()


def body(
    grid_input, w_hidden, b_hidden, w_out, b_out, target, channel_weight, interp_weight, block_index
):
    V = pltpu.VMEM
    D = pltpu.SemaphoreType.DMA
    any_spec = pl.BlockSpec(memory_space=pl.ANY)
    vmem_spec = pl.BlockSpec(memory_space=pltpu.VMEM)
    scratch = [
        V((4, 4, 128, 1024), BF16), V((1024, 1024), BF16), V((1024, 1024), BF16),
        V((96, 1024), BF16),
        V((4, 3, 128, 128), BF16), V((96, 128), F32),
        V((4, 4, 128, 1024), BF16), V((4, 4, 128, 1024), F32), V((4, 4, 128, 1024), BF16),
        V((768, 512), BF16), V((128, 128), F32), V((128, 128), F32),
        V((4, 4, 96, 128), BF16), V((3, 4, 96, 128), BF16),
        V((16, 96, 128), F32), V((16, 96, 128), F32),
        V((4, 3, 96, 128), BF16), V((4, 4, 96, 128), BF16), V((128, 1024), F32),
        V((4, 2, 256, 512), BF16), V((4, 2, 256, 512), BF16),
        V((4, 2, 256, 512), BF16), V((4, 2, 256, 512), BF16),
        V((2, 4, 4, 32, CW), F32), V((4, 4, 32, CW), BF16), V((4, 4, 32, CW), BF16),
        V((4, 4, 32, CW), BF16), V((6, 2, 32, CW), BF16), V((2, 2, 32, CW), BF16),
        V((4, 32, CW), F32), V((4, 32, CW), BF16), V((3, 32, CW), BF16),
        V((4, 8, CW), F32), V((3, 8, CW), F32),
        D((4,)), D((4,)), D((3,)), D((3,)), D((4, 3)), D((4, 3)),
        D((4, 2)), D((4, 2)), D((4, 2)), D((4, 2)), D((4,)), D((4,)),
        D((6,)), D((6,)), D((3,)), D((3,)), D((3,)), D((3,)),
    ]
    held = pl.pallas_call(
        kernel,
        out_shape=(V((8, 1024), F32), V((8, 128), F32), V((4, 256, 1024), F32)),
        in_specs=[any_spec] * 3 + [vmem_spec] * 3 + [any_spec] * 2
        + [pl.BlockSpec(memory_space=pltpu.SMEM)],
        out_specs=(vmem_spec, vmem_spec, vmem_spec),
        scratch_shapes=scratch,
        compiler_params=pltpu.CompilerParams(
            collective_id=0, has_side_effects=True, vmem_limit_bytes=54 * 2**20
        ),
    )(
        grid_input, w_hidden, w_out.T, b_hidden[None], b_out[None], channel_weight[None],
        target, interp_weight, block_index,
    )
    held = [pltpu.with_memory_space_constraint(h, pltpu.VMEM) for h in held]
    return pl.pallas_call(
        store,
        out_shape=(
            jax.ShapeDtypeStruct((8, 1024), F32),
            jax.ShapeDtypeStruct((8, 96), F32),
            jax.ShapeDtypeStruct((4, 256, 1024), F32),
        ),
        in_specs=[vmem_spec] * 3,
        out_specs=(vmem_spec, vmem_spec, any_spec),
        scratch_shapes=[D((4,))],
        compiler_params=pltpu.CompilerParams(vmem_limit_bytes=2**20),
    )(*held)


def solution(mesh):
    placed = (
        P("member", "region", None),
        P(),
        P(),
        P(),
        P(),
        P(None, "region"),
        P(),
        P("region", None, None, None),
        P("region", None),
    )
    return jax.shard_map(
        body,
        mesh=mesh,
        in_specs=placed,
        out_specs=(
            P(("member", "region"), None),
            P(("member", "region"), None),
            P("member", "region", None),
        ),
        check_vma=False,
    )
```

```python
import jax
import jax.numpy as jnp
from jax import lax
from jax.experimental import pallas as pl
from jax.experimental.pallas import tpu as pltpu
from jax.sharding import PartitionSpec as P

MESH = pl.DeviceIdType.MESH
F32 = jnp.float32
BF16 = jnp.bfloat16
M = 16
ALPHA = 0.95
SMOOTH = 0.25
KAPPA = ALPHA / (2.0 * M * (M - 1)) + (1.0 - ALPHA) / (2.0 * M * M)
CW = 1152
PARTS = (slice(0, 640), slice(640, CW))


def kernel(
    x_hbm, wh_hbm, wot_hbm, bh_ref, bo_ref, cw_ref, tgt_hbm, tile_hbm, bi_ref,
    gh_ref, go_ref, own,
    xv, wh, wht, wot, tiles, tgt, act, dsil, dpre, wt, bcol, ccol,
    predsend, predrecv, pf, adjf, adjsend, adjrecv, outt,
    send_dn, send_up, recv_dn, recv_up,
    accf, csend, crecv, s1, ring_in, onward, p2, s2, r2, p3, s3, r3,
    load_sem, x_sem, pred_ss, pred_rs, adj_ss, adj_rs, dn_ss, dn_rs, up_ss, up_rs,
    c_ss, c_rs, ring_ss, ring_rs, y_ss, y_rs, x_ss, x_rs,
):
    z = lax.axis_index("member")
    r = lax.axis_index("region")
    yy, xx, cc = r // 8, (r // 2) % 4, r % 2
    oc = 1 - cc

    def zdev(k):
        return ((z + k) % 4, r)

    def ydev(k):
        return (z, ((yy + k) % 4) * 8 + xx * 2 + cc)

    def xdev(k):
        return (z, yy * 8 + ((xx + k) % 4) * 2 + cc)

    partner = (z, r + 1 - 2 * cc)
    up = (z, (r + 1) % 32)
    down = (z, (r + 31) % 32)

    def block_of(i):
        return (z + 1 + i) % 4

    barrier = pltpu.get_barrier_semaphore()
    peers = [f(k) for f in (zdev, ydev, xdev) for k in (1, 2, 3)] + [up, down]
    for peer in peers:
        pl.semaphore_signal(barrier, inc=1, device_id=peer, device_id_type=MESH)

    load_wh = pltpu.make_async_copy(wh_hbm, wh, load_sem.at[0])
    load_wh.start()

    def x_copy(i):
        start = pl.multiple_of(block_of(i) * 128, 128)
        return pltpu.make_async_copy(
            x_hbm.at[:, pl.ds(start, 128), :], xv.at[i], x_sem.at[i]
        )

    x_copy(0).start()
    load_wot = pltpu.make_async_copy(wot_hbm, wot, load_sem.at[1])
    load_wot.start()
    for i in range(1, 4):
        x_copy(i).start()
    load_tiles = pltpu.make_async_copy(tile_hbm, tiles, load_sem.at[2])
    load_tiles.start()
    load_tgt = pltpu.make_async_copy(
        tgt_hbm.at[:, pl.ds(pl.multiple_of(z * 128, 128), 128)], tgt, load_sem.at[3]
    )
    load_tgt.start()

    def pred_copy(i):
        return pltpu.make_async_remote_copy(
            src_ref=predsend.at[i], dst_ref=predrecv.at[i],
            send_sem=pred_ss.at[i], recv_sem=pred_rs.at[i],
            device_id=zdev(i + 1), device_id_type=MESH,
        )

    load_wot.wait()
    load_wh.wait()

    def forward(i, carry):
        x_copy(i).wait()
        xb = xv[i].reshape(512, 1024)
        for n in range(4):
            cols = slice(n * 256, n * 256 + 256)
            pre = jnp.dot(xb, wh[:, cols], preferred_element_type=F32) + bh_ref[:, cols]
            sig = 0.5 + 0.5 * jnp.tanh(0.5 * pre)
            silu = pre * sig
            act[i, :, :, cols] = silu.astype(BF16).reshape(4, 128, 256)
            dsil[i, :, :, cols] = (sig + silu * (1.0 - sig)).reshape(4, 128, 256)
        predt = lax.dot_general(
            wot[...], act[i].reshape(512, 1024), (((1,), (1,)), ((), ())),
            preferred_element_type=F32,
        ).astype(BF16)
        for m in range(4):
            predsend[i, m] = predt[:, m * 128 : m * 128 + 128]

        @pl.when(i == 0)
        def _():
            pl.semaphore_wait(barrier, len(peers))

        @pl.when(i < 3)
        def _():
            pred_copy(i).start()

        return carry

    lax.fori_loop(0, 4, forward, 0)

    load_tiles.wait()

    def build(i, carry):
        b = block_of(i)
        place = pl.ds(pl.multiple_of(i * 128, 128), 128)
        slots = []
        turned = []
        for k in range(3):
            index = bi_ref[b, k]
            relative = (index // 2 - r + 33) % 32
            slots.append(relative * 2 + index % 2)
            turned.append(tiles[b, k].astype(F32).T)
        for s in range(6):
            total = None
            for k in range(3):
                term = turned[k] * jnp.where(slots[k] == s, 1.0, 0.0)
                total = term if total is None else total + term
            wt[s * 128 : s * 128 + 128, place] = total.astype(BF16)
        return carry

    lax.fori_loop(0, 4, build, 0)

    bcol[...] = jnp.zeros_like(bcol)
    ccol[...] = jnp.zeros_like(ccol)
    bcol[:, :96] = jnp.broadcast_to(bo_ref[...], (128, 96))
    ccol[:, :96] = jnp.broadcast_to(cw_ref[...], (128, 96))
    bcol[...] = bcol[...].T
    ccol[...] = ccol[...].T
    load_tgt.wait()

    pf[12:16] = predsend[3].astype(F32)
    for i in range(3):
        pred_copy(i).wait_recv()
        pf[4 * i : 4 * i + 4] = predrecv[i].astype(F32)

    def score(t, carry):
        rows = pl.ds(pl.multiple_of(t * 8, 8), 8)
        p = pf[:, rows, :]
        aim = tgt[rows, :] - bcol[rows, :]

        def slope(d):
            return d * lax.rsqrt(d * d + SMOOTH * SMOOTH)

        spread = None
        for k in range(1, 8):
            s = slope(p - jnp.concatenate([p[k:], p[:k]], axis=0))
            change = s - jnp.concatenate([s[16 - k :], s[: 16 - k]], axis=0)
            spread = change if spread is None else spread + change
        s = slope(p[:8] - p[8:])
        spread = spread + jnp.concatenate([s, -s], axis=0)
        skill = slope(p - aim[None])
        adjf[:, rows, :] = ccol[rows, :][None] * (skill * (1.0 / M) - 2.0 * KAPPA * spread)
        return carry

    lax.fori_loop(0, 12, score, 0)

    def adj_copy(m, i):
        return pltpu.make_async_remote_copy(
            src_ref=adjsend.at[m, i], dst_ref=adjrecv.at[m, i],
            send_sem=adj_ss.at[m, i], recv_sem=adj_rs.at[m, i],
            device_id=zdev(3 - i), device_id_type=MESH,
        )

    for m in range(4):
        for i in range(3):
            adjsend[m, i] = adjf[4 * i + m].astype(BF16)
            adj_copy(m, i).start()
        adjrecv[m, 3] = adjf[12 + m].astype(BF16)

    def dn_copy(m, h):
        return pltpu.make_async_remote_copy(
            src_ref=send_dn.at[m, h], dst_ref=recv_dn.at[m, h],
            send_sem=dn_ss.at[m, h], recv_sem=dn_rs.at[m, h],
            device_id=down, device_id_type=MESH,
        )

    def up_copy(m, h):
        return pltpu.make_async_remote_copy(
            src_ref=send_up.at[m, h], dst_ref=recv_up.at[m, h],
            send_sem=up_ss.at[m, h], recv_sem=up_rs.at[m, h],
            device_id=up, device_id_type=MESH,
        )

    outt[...] = jnp.zeros_like(outt)
    for n in range(4):
        wht[:, n * 256 : n * 256 + 256] = wh[n * 256 : n * 256 + 256, :].T

    def hidden(m):
        for i in range(3):
            adj_copy(m, i).wait_recv()
        adj = jnp.concatenate([adjrecv[m, i] for i in range(4)], axis=1)
        for n in range(4):
            cols = slice(n * 256, n * 256 + 256)
            dact = lax.dot_general(
                adj, wot[:, cols], (((0,), (0,)), ((), ())), preferred_element_type=F32
            )
            grad = dact * dsil[:, m, :, cols].reshape(512, 256)
            dpre[:, m, :, cols] = grad.astype(BF16).reshape(4, 128, 256)
        outt[:96, :] += jnp.dot(
            adj, act[:, m].reshape(512, 1024), preferred_element_type=F32
        )

    def interpolate(m):
        dp = dpre[:, m].reshape(512, 1024)
        for h in range(2):
            cols = slice(h * 512, h * 512 + 512)
            dinput = jnp.dot(dp, wht[:, cols], preferred_element_type=F32).astype(BF16)
            contrib = jnp.dot(wt[...], dinput, preferred_element_type=F32)
            send_dn[m, h] = contrib[:256].astype(BF16)
            own[m, :, cols] = contrib[256:512]
            send_up[m, h] = contrib[512:].astype(BF16)
            if h == 0:
                dn_copy(m, h).start()
                up_copy(m, h).start()
            else:

                @pl.when(m < 3)
                def _():
                    dn_copy(m, 1).start()
                    up_copy(m, 1).start()

    def first_half(m, carry):
        hidden(m)
        interpolate(m)
        return carry

    def second_half(m, carry):
        hidden(m)
        return carry

    lax.fori_loop(0, 2, first_half, 0)
    lax.fori_loop(2, 4, second_half, 0)

    turned_out = outt[...].T.reshape(4, 4, 4, 2, 8, 128)
    for c in range(2):
        accf[c, :, :, :, 1024:] = turned_out[:, :, :, c].reshape(4, 4, 32, 128)

    def row_of(j):
        return (z + 2 + j + (j // 2) * (2 * j - 3)) % 4

    def c_copy(j):
        return pltpu.make_async_remote_copy(
            src_ref=csend.at[j], dst_ref=crecv.at[j],
            send_sem=c_ss.at[j], recv_sem=c_rs.at[j],
            device_id=partner, device_id_type=MESH,
        )

    def gradient(j):
        zc = row_of(j)
        start = pl.multiple_of(zc * 256, 256)
        lhs = xv[:, :, :, pl.ds(start, 256)].reshape(2048, 256)
        for n in range(2):
            cols = slice(n * 512, n * 512 + 512)
            part = lax.dot_general(
                lhs, dpre[:, :, :, cols].reshape(2048, 512), (((0,), (0,)), ((), ())),
                preferred_element_type=F32,
            ).reshape(4, 4, 2, 8, 512)
            for c in range(2):
                accf[c, zc, :, :, cols] = part[:, :, c].reshape(4, 32, 512)
        csend[j] = accf[oc, zc].astype(BF16)
        c_copy(j).start()

    def combine(j):
        zc = row_of(j)
        c_copy(j).wait_recv()
        total = accf[cc, zc] + crecv[j].astype(F32)
        accf[cc, zc] = total
        s1[zc] = total.astype(BF16)

    after, before, far = (z + 1) % 4, (z + 3) % 4, (z + 2) % 4
    low, high = slice(0, 2), slice(2, 4)

    def ring(n, h):
        cols = PARTS[h]
        src, dst, k = (
            (s1.at[far, low, :, cols], ring_in.at[0, :, :, cols], 1),
            (s1.at[far, high, :, cols], ring_in.at[1, :, :, cols], 3),
            (s1.at[after, high, :, cols], ring_in.at[2, :, :, cols], 1),
            (s1.at[before, low, :, cols], ring_in.at[3, :, :, cols], 3),
            (onward.at[0, :, :, cols], ring_in.at[4, :, :, cols], 1),
            (onward.at[1, :, :, cols], ring_in.at[5, :, :, cols], 3),
        )[n]
        return pltpu.make_async_remote_copy(
            src_ref=src, dst_ref=dst, send_sem=ring_ss.at[n, h], recv_sem=ring_rs.at[n, h],
            device_id=zdev(k), device_id_type=MESH,
        )

    def y2(k, h):
        return pltpu.make_async_remote_copy(
            src_ref=s2.at[(yy + k) % 4, :, PARTS[h]], dst_ref=r2.at[k - 1, :, PARTS[h]],
            send_sem=y_ss.at[k - 1, h], recv_sem=y_rs.at[k - 1, h],
            device_id=ydev(k), device_id_type=MESH,
        )

    def x3(k, h):
        return pltpu.make_async_remote_copy(
            src_ref=s3.at[(xx + k) % 4, :, PARTS[h]], dst_ref=r3.at[k - 1, :, PARTS[h]],
            send_sem=x_ss.at[k - 1, h], recv_sem=x_rs.at[k - 1, h],
            device_id=xdev(k), device_id_type=MESH,
        )

    def weights(j, carry):
        gradient(j)

        @pl.when(j == 2)
        def _():
            combine(0)
            for h in range(2):
                ring(0, h).start()
                ring(1, h).start()

        @pl.when(j == 3)
        def _():
            combine(1)
            ring(3, 0).start()

        return carry

    lax.fori_loop(0, 4, weights, 0)

    def pass_on(h):
        cols = PARTS[h]
        ring(0, h).wait_recv()
        total = accf[cc, after, low, :, cols] + ring_in[0, :, :, cols].astype(F32)
        onward[0, :, :, cols] = total.astype(BF16)
        ring(4, h).start()
        ring(1, h).wait_recv()
        total = accf[cc, before, high, :, cols] + ring_in[1, :, :, cols].astype(F32)
        onward[1, :, :, cols] = total.astype(BF16)
        ring(5, h).start()

    combine(2)
    ring(2, 0).start()

    def last(m, carry):
        interpolate(m)

        @pl.when(m == 2)
        def _():
            combine(3)
            pass_on(0)
            ring(2, 1).start()
            ring(3, 1).start()
            pass_on(1)

        return carry

    lax.fori_loop(2, 4, last, 0)

    def finish(m, carry):
        for h in range(2):
            cols = slice(h * 512, h * 512 + 512)
            dn_copy(m, h).wait_recv()
            up_copy(m, h).wait_recv()
            own[m, :, cols] = (
                own[m, :, cols] + recv_dn[m, h].astype(F32) + recv_up[m, h].astype(F32)
            )
        return carry

    lax.fori_loop(0, 1, finish, 0)
    for h in range(2):
        cols = PARTS[h]
        for n in range(2, 6):
            ring(n, h).wait_recv()
        first = accf[cc, z, low, :, cols] + ring_in[4, :, :, cols].astype(F32)
        first = first + ring_in[3, :, :, cols].astype(F32)
        second = accf[cc, z, high, :, cols] + ring_in[5, :, :, cols].astype(F32)
        second = second + ring_in[2, :, :, cols].astype(F32)
        p2[0:2, :, cols] = first
        p2[2:4, :, cols] = second
        s2[0:2, :, cols] = first.astype(BF16)
        s2[2:4, :, cols] = second.astype(BF16)
        for k in (2, 1, 3):
            y2(k, h).start()

    for h in range(2):
        cols = PARTS[h]
        for k in (1, 3, 2):
            y2(k, h).wait_recv()
        total = p2[yy, :, cols]
        for k in range(3):
            total = total + r2[k, :, cols].astype(F32)
        total = total.reshape(4, 8, cols.stop - cols.start)
        p3[:, :, cols] = total
        s3[:, :, cols] = total.astype(BF16)
        for k in (2, 1, 3):
            x3(k, h).start()
    dn_copy(3, 1).start()
    up_copy(3, 1).start()
    lax.fori_loop(1, 3, finish, 0)

    for k in (1, 3, 2):
        for h in range(2):
            x3(k, h).wait_recv()
    total = p3[xx]
    for k in range(3):
        total = total + r3[k].astype(F32)
    gh_ref[...] = total[:, :1024]
    go_ref[...] = total[:, 1024:]

    lax.fori_loop(3, 4, finish, 0)

    for i in range(3):
        pred_copy(i).wait_send()
        for m in range(4):
            adj_copy(m, i).wait_send()
    for m in range(4):
        for h in range(2):
            dn_copy(m, h).wait_send()
            up_copy(m, h).wait_send()
        c_copy(m).wait_send()
    for k in (1, 2, 3):
        for f in (y2, x3):
            for h in range(2):
                f(k, h).wait_send()
    for n in range(6):
        for h in range(2):
            ring(n, h).wait_send()


def store(gh_ref, go_ref, mesh_ref, gh_out, go_out, mesh_out, sem):
    copies = [pltpu.make_async_copy(mesh_ref.at[m], mesh_out.at[m], sem.at[m]) for m in range(4)]
    for copy in copies:
        copy.start()
    gh_out[...] = gh_ref[...]
    go_out[...] = go_ref[:, :96]
    for copy in copies:
        copy.wait()


def body(
    grid_input, w_hidden, b_hidden, w_out, b_out, target, channel_weight, interp_weight, block_index
):
    V = pltpu.VMEM
    D = pltpu.SemaphoreType.DMA
    any_spec = pl.BlockSpec(memory_space=pl.ANY)
    vmem_spec = pl.BlockSpec(memory_space=pltpu.VMEM)
    scratch = [
        V((4, 4, 128, 1024), BF16), V((1024, 1024), BF16), V((1024, 1024), BF16),
        V((96, 1024), BF16),
        V((4, 3, 128, 128), BF16), V((96, 128), F32),
        V((4, 4, 128, 1024), BF16), V((4, 4, 128, 1024), F32), V((4, 4, 128, 1024), BF16),
        V((768, 512), BF16), V((128, 128), F32), V((128, 128), F32),
        V((4, 4, 96, 128), BF16), V((3, 4, 96, 128), BF16),
        V((16, 96, 128), F32), V((16, 96, 128), F32),
        V((4, 3, 96, 128), BF16), V((4, 4, 96, 128), BF16), V((128, 1024), F32),
        V((4, 2, 256, 512), BF16), V((4, 2, 256, 512), BF16),
        V((4, 2, 256, 512), BF16), V((4, 2, 256, 512), BF16),
        V((2, 4, 4, 32, CW), F32), V((4, 4, 32, CW), BF16), V((4, 4, 32, CW), BF16),
        V((4, 4, 32, CW), BF16), V((6, 2, 32, CW), BF16), V((2, 2, 32, CW), BF16),
        V((4, 32, CW), F32), V((4, 32, CW), BF16), V((3, 32, CW), BF16),
        V((4, 8, CW), F32), V((4, 8, CW), BF16), V((3, 8, CW), BF16),
        D((4,)), D((4,)), D((3,)), D((3,)), D((4, 3)), D((4, 3)),
        D((4, 2)), D((4, 2)), D((4, 2)), D((4, 2)), D((4,)), D((4,)),
        D((6, 2)), D((6, 2)), D((3, 2)), D((3, 2)), D((3, 2)), D((3, 2)),
    ]
    held = pl.pallas_call(
        kernel,
        out_shape=(V((8, 1024), F32), V((8, 128), F32), V((4, 256, 1024), F32)),
        in_specs=[any_spec] * 3 + [vmem_spec] * 3 + [any_spec] * 2
        + [pl.BlockSpec(memory_space=pltpu.SMEM)],
        out_specs=(vmem_spec, vmem_spec, vmem_spec),
        scratch_shapes=scratch,
        compiler_params=pltpu.CompilerParams(
            collective_id=0, has_side_effects=True, vmem_limit_bytes=54 * 2**20
        ),
    )(
        grid_input, w_hidden, w_out.T, b_hidden[None], b_out[None], channel_weight[None],
        target, interp_weight, block_index,
    )
    held = [pltpu.with_memory_space_constraint(h, pltpu.VMEM) for h in held]
    return pl.pallas_call(
        store,
        out_shape=(
            jax.ShapeDtypeStruct((8, 1024), F32),
            jax.ShapeDtypeStruct((8, 96), F32),
            jax.ShapeDtypeStruct((4, 256, 1024), F32),
        ),
        in_specs=[vmem_spec] * 3,
        out_specs=(vmem_spec, vmem_spec, any_spec),
        scratch_shapes=[D((4,))],
        compiler_params=pltpu.CompilerParams(vmem_limit_bytes=2**20),
    )(*held)


def solution(mesh):
    placed = (
        P("member", "region", None),
        P(),
        P(),
        P(),
        P(),
        P(None, "region"),
        P(),
        P("region", None, None, None),
        P("region", None),
    )
    return jax.shard_map(
        body,
        mesh=mesh,
        in_specs=placed,
        out_specs=(
            P(("member", "region"), None),
            P(("member", "region"), None),
            P("member", "region", None),
        ),
        check_vma=False,
    )
```
